512 devices in a mesh: ctx: 128 (over z_hi, y, x, core), head: 4 (over z_lo).
Axes of the slice: x: 4, y: 4, z: 16 (z_hi: 4, z_lo: 4; z = z_hi * 4 + z_lo), core: 2. Of those that a mesh axis runs over, the one named last changes fastest.
Arguments:
- queries: bfloat16 [32768, 2048], P(('ctx', 'head')), may hold values from -8.5 to 8.5
- keys: bfloat16 [32768, 1024], P(('ctx', 'head')), may hold values from -8.5 to 8.5
- values: bfloat16 [32768, 1024], P(('ctx', 'head')), may hold values from -5 to 5
- grad_attn: bfloat16 [32768, 2048], P(('ctx', 'head')), may hold values from -5 to 5
- parent_gap: int32 [128], replicated, may hold values from 0 to 2, as said below
Outputs:
- attended: bfloat16 [32768, 2048], P(('ctx', 'head'))
- grad_query: bfloat16 [32768, 2048], P(('ctx', 'head'))
- grad_key: bfloat16 [32768, 1024], P(('ctx', 'head'))
- grad_value: bfloat16 [32768, 1024], P(('ctx', 'head'))
The draws below stay inside these ranges and needn't reach their ends.
Inputs may be any that keep to these rules, and one draw needn't show every extreme that they name: Shards are in depth-first order of a tree rooted at shard 0: the parent of shard s > 0 is shard s - parent_gap[s], and parent_gap[0] = 0. The ancestor 4 levels above a shard, where it exists, lies at most 8 shards before it.
All inputs are finite; a program needn't handle non-finite values.
Results may differ from the reference program's by a relative error of at most 0.011.
Values may be sent and summed in bfloat16 or wider, within the bound.
No kernel may reach another device: no remote copies, remote signals or barrier semaphores. Data moves between devices by JAX's collectives and lax.ppermute only.
A program may use at most 64 MiB of HBM per device.

```python
import math
import jax
import jax.numpy as jnp
from jax import lax

HD = 256
KVH = 4
GROUP = 2
FORK = 2
TOK_DEV = 256
QH = 8
LEVELS = 4
SHARDS = 128
TOKENS = 32768


def query_key_pair(key):
    shape_query = (TOKENS, KVH, GROUP, HD)
    shape_key = (TOKENS, KVH, HD)
    query = jax.random.truncated_normal(jax.random.fold_in(key, 21), -4.0, 4.0, shape_query, jnp.float32)
    key_base = jax.random.truncated_normal(jax.random.fold_in(key, 22), -4.0, 4.0, shape_key, jnp.float32)
    return (query.reshape(TOKENS, KVH * GROUP * HD), key_base.reshape(TOKENS, KVH * HD))


def draw_queries(key, part):
    return query_key_pair(key)[0].astype(jnp.bfloat16)


def draw_keys(key, part):
    return query_key_pair(key)[1].astype(jnp.bfloat16)


def draw_parent_gap(key, part):
    leaves = jax.random.randint(jax.random.fold_in(key, 31), (SHARDS,), 0, FORK)
    leeway = (SHARDS - 1) // FORK - LEVELS + 1
    forced_start = jax.random.randint(jax.random.fold_in(key, 32), (), 0, leeway)
    ordinal = jnp.arange(SHARDS, dtype=jnp.int32)
    forced = jnp.logical_and(ordinal >= forced_start, ordinal < forced_start + LEVELS)
    leaves = jnp.where(forced, FORK - 1, leaves)
    length = leaves + 1
    starts = jnp.cumsum(length) - length
    member = jnp.sum((starts[None, :] <= ordinal[:, None]).astype(jnp.int32), 1) - 1
    within = ordinal - jnp.take(starts, member)
    before = jnp.take(length, jnp.maximum(member - 1, 0))
    gaps = jnp.where(within > 0, within, jnp.where(member > 0, before, 0))
    return gaps.astype(jnp.int32)


def block_scale(key, dims, cuts, least, top_value):
    factor_of = 1.0
    for dim, blocks in cuts:
        heights = jax.random.uniform(jax.random.fold_in(jax.random.fold_in(key, 6), dim), (blocks,), jnp.float32, least / len(cuts), top_value / len(cuts))
        factor_of = factor_of * jnp.repeat(jnp.exp(heights), dims[dim] // blocks).reshape((-1,) + (1,) * (len(dims) - 1 - dim))
    return factor_of


def normal_values(own_key, shape, scale, limit, split=(), held_as=jnp.bfloat16):
    gain = block_scale(own_key, shape, split, -0.22, 0.18) if split else 1.0
    entries = jax.random.normal(own_key, shape, jnp.float32) * scale * gain
    return jnp.minimum(jnp.maximum(entries, -limit), limit).astype(held_as)


def setup_inputs(seed: int = 0) -> dict:
    splits = jax.random.split(jax.random.key(seed), 6)
    queries = draw_queries(jax.random.fold_in(splits[5], 71), 0)
    keys = draw_keys(jax.random.fold_in(splits[5], 71), 0)
    values = normal_values(splits[2], (TOKENS, KVH * HD), 1.0, 5.0, ((0, 512),))
    grad_attn = normal_values(splits[3], (TOKENS, QH * HD), 1.0, 5.0, ((0, 512),))
    parent_gap = draw_parent_gap(jax.random.fold_in(splits[5], 71), 0)
    return dict(queries=queries, keys=keys, values=values, grad_attn=grad_attn, parent_gap=parent_gap)


BASE = 10000.0


def tree_tables(parent_gap):
    shard_count = parent_gap.shape[0]
    ordinal = jnp.arange(shard_count, dtype=jnp.int32)
    parent = jnp.where(parent_gap > 0, ordinal - parent_gap, shard_count).astype(jnp.int32)
    pointer = jnp.concatenate([parent, jnp.full((1,), shard_count, jnp.int32)])
    depths = jnp.concatenate([(parent_gap > 0).astype(jnp.int32), jnp.zeros((1,), jnp.int32)])
    jumped = pointer
    for rounds in range(shard_count.bit_length()):
        depths = depths + jnp.take(depths, jumped)
        jumped = jnp.take(jumped, jumped)
    return pointer, depths


def rotate(inputs, position, direction):
    half_dim = inputs.shape[-1] // 2
    frequency = jnp.exp(jnp.arange(half_dim, dtype=jnp.float32) * (-2.0 * math.log(BASE) / inputs.shape[-1]))
    angles = position.astype(jnp.float32)[:, None] * frequency[None, :]
    cosine = jnp.cos(angles)[:, None, :]
    sine_part = direction * jnp.sin(angles)[:, None, :]
    first_half = inputs[..., :half_dim]
    second = inputs[..., half_dim:]
    return jnp.concatenate([first_half * cosine - second * sine_part, second * cosine + first_half * sine_part], -1)


def visible_mask(length, levels, present):
    within = jnp.arange(length, dtype=jnp.int32)
    later_key = within[None, :] > within[:, None]
    blocks_list = [jnp.logical_not(later_key)]
    for height in range(1, levels + 1):
        blocks_list.append(jnp.logical_and(present[height - 1], jnp.logical_or(height < levels, later_key)))
    return jnp.stack(blocks_list, 1).reshape(length, (levels + 1) * length)


def attend_exact(query, key_all, value_all, grad_out, visible):
    scaling = query.shape[-1] ** -0.5
    query32 = query.astype(jnp.float32)
    key32 = key_all.astype(jnp.float32)
    value32 = value_all.astype(jnp.float32)
    grad32 = grad_out.astype(jnp.float32)
    scores = jnp.einsum("tkgd,ukd->kgtu", query32, key32) * scaling
    scores = jnp.where(visible, scores, -1e30)
    highest = jnp.max(scores, -1, keepdims=True)
    raw_weights = jnp.where(visible, jnp.exp(scores - highest), 0.0)
    probabilities = raw_weights / jnp.sum(raw_weights, -1, keepdims=True)
    probs_low = probabilities.astype(jnp.bfloat16)
    attended = jnp.einsum("kgtu,ukd->tkgd", probs_low.astype(jnp.float32), value32).astype(jnp.bfloat16)
    grad_prob = jnp.einsum("tkgd,ukd->kgtu", grad32, value32)
    row_delta = jnp.sum(probabilities * grad_prob, -1, keepdims=True)
    grad_score = (probabilities * (grad_prob - row_delta) * scaling).astype(jnp.bfloat16)
    score32 = grad_score.astype(jnp.float32)
    grad_qrot = jnp.einsum("kgtu,ukd->tkgd", score32, key32)
    part_key = jnp.einsum("kgtu,tkgd->ukd", score32, query32)
    part_value = jnp.einsum("kgtu,tkgd->ukd", probs_low.astype(jnp.float32), grad32)
    return attended, grad_qrot, part_key, part_value


def reference(queries, keys, values, grad_attn, parent_gap):
    pointer, depths = tree_tables(parent_gap)
    ordinal = jnp.arange(SHARDS, dtype=jnp.int32)
    elders = []
    current = pointer[:SHARDS]
    for height in range(LEVELS):
        elders.append(current)
        current = jnp.take(pointer, current)
    elders = jnp.stack(elders, 1)
    present = elders < SHARDS
    table = jnp.concatenate([ordinal[:, None], jnp.where(present, elders, 0)], 1).astype(jnp.int32)
    within = jnp.arange(TOK_DEV, dtype=jnp.int32)
    position = (depths[:SHARDS, None] * TOK_DEV + within[None, :]).reshape(TOKENS)
    query_rot = rotate(queries.astype(jnp.float32).reshape(TOKENS, QH, HD), position, 1.0).astype(jnp.bfloat16)
    query_rot = query_rot.reshape(SHARDS, TOK_DEV, KVH, GROUP, HD)
    key_rot = rotate(keys.astype(jnp.float32).reshape(TOKENS, KVH, HD), position, 1.0).astype(jnp.bfloat16)
    key_rot = key_rot.reshape(SHARDS, TOK_DEV, KVH, HD)
    value_shards = values.reshape(SHARDS, TOK_DEV, KVH, HD)
    grad_shards = grad_attn.reshape(SHARDS, TOK_DEV, KVH, GROUP, HD)
    shard_positions = position.reshape(SHARDS, TOK_DEV)

    def shard_step(carry, shard_id):
        total_key, total_value = carry
        chosen = table[shard_id]
        key_all = jnp.take(key_rot, chosen, axis=0).reshape((LEVELS + 1) * TOK_DEV, KVH, HD)
        value_all = jnp.take(value_shards, chosen, axis=0).reshape((LEVELS + 1) * TOK_DEV, KVH, HD)
        visible = visible_mask(TOK_DEV, LEVELS, present[shard_id])
        attended, grad_qrot, part_key, part_value = attend_exact(query_rot[shard_id], key_all, value_all, grad_shards[shard_id], visible)
        total_key = total_key.at[chosen].add(part_key.reshape(LEVELS + 1, TOK_DEV, KVH, HD))
        total_value = total_value.at[chosen].add(part_value.reshape(LEVELS + 1, TOK_DEV, KVH, HD))
        grad_query = rotate(grad_qrot.reshape(TOK_DEV, QH, HD), shard_positions[shard_id], -1.0).astype(jnp.bfloat16)
        return (total_key, total_value), (attended.reshape(TOK_DEV, QH * HD), grad_query.reshape(TOK_DEV, QH * HD))

    zeros = jnp.zeros((SHARDS, TOK_DEV, KVH, HD), jnp.float32)
    (total_key, total_value), (attended, grad_query) = lax.scan(shard_step, (zeros, zeros), ordinal)
    grad_key = rotate(total_key.reshape(TOKENS, KVH, HD), position, -1.0).astype(jnp.bfloat16).reshape(TOKENS, KVH * HD)
    grad_value = total_value.astype(jnp.bfloat16).reshape(TOKENS, KVH * HD)
    return attended.reshape(TOKENS, QH * HD), grad_query.reshape(TOKENS, QH * HD), grad_key, grad_value
```

```python
import functools
import math

import jax
import jax.numpy as jnp
from jax import lax
from jax.experimental import pallas as pl
from jax.experimental.pallas import tpu as pltpu
from jax.sharding import Mesh
from jax.sharding import PartitionSpec as P

HD = 256
HALF = HD // 2
TOK = 256
LEVELS = 4
SLOTS = LEVELS + 1
CHIPS = 4
CORES = 2
PAIR = CORES * TOK
ROW = CHIPS * CORES
HEADS = 4
BASE = 10000.0
BF16 = jnp.bfloat16
F32 = jnp.float32

ANY = pl.BlockSpec(memory_space=pl.ANY)
VMEM = pl.BlockSpec(memory_space=pltpu.VMEM)
SMEM = pl.BlockSpec(memory_space=pltpu.SMEM)


def plan(parent_gap, row, chip, core):
    count = parent_gap.shape[0]
    ordinal = jnp.arange(count, dtype=jnp.int32)
    deeper = (parent_gap == 1).astype(jnp.int32)
    depths = jnp.sum(jnp.where(ordinal[None, :] <= ordinal[:, None], deeper[None, :], 0), 1)
    shard = row * ROW + chip * CORES + core
    first = row * ROW
    asked = jnp.stack([shard, shard + 1 - 2 * core, first, first + ROW])
    own_depth = jnp.sum(
        jnp.where(ordinal[None, :] <= asked[:, None], deeper[None, :], 0), 1
    ) + (asked >= count)
    wanted = own_depth[:, None] - jnp.arange(1, SLOTS, dtype=jnp.int32)[None, :]
    match = (depths[None, None, :] == wanted[:, :, None]) & (
        ordinal[None, None, :] < asked[:, None, None]
    )
    elder = jnp.max(jnp.where(match, ordinal[None, None, :], -1), 2)
    present = (elder >= 0).astype(jnp.int32)

    def place(node):
        return 2 * ((chip - (node - first) // CORES) % CHIPS) + node % CORES

    mine = elder[:2]
    rank = jnp.sum(
        jnp.where(mine[:, :, None] == elder[2][None, None, :], jnp.arange(LEVELS, dtype=jnp.int32), 0),
        2,
    )
    code = jnp.where(mine >= first, place(mine), 2 * CHIPS + (chip - rank) % CHIPS)
    code = jnp.where(mine >= 0, code, 0)
    code = jnp.concatenate([jnp.stack([core, 1 - core])[:, None], code], 1)
    relay = jnp.clip(elder[3], first, first + ROW - 1)
    relay_code = place(relay)
    holder = (chip - jnp.arange(CHIPS, dtype=jnp.int32)) % CHIPS
    sent = jnp.sum(jnp.where(jnp.arange(LEVELS) == chip, relay_code, 0))
    landing = jnp.sum(
        jnp.where(holder[:, None] == jnp.arange(LEVELS)[None, :], relay_code[None, :], 0), 1
    )
    table = jnp.concatenate(
        [code.reshape(-1), present[0], sent[None], landing, core[None]]
    ).astype(jnp.int32)
    pair_depth = jnp.sum(
        jnp.where(
            ordinal[None, :] <= (first + chip * CORES + jnp.arange(CORES))[:, None],
            deeper[None, :],
            0,
        ),
        1,
    )
    return table, pair_depth


def angles_of(depth):
    frequency = jnp.exp(jnp.arange(HALF, dtype=F32) * (-2.0 * math.log(BASE) / HD))
    position = (depth[:, None] * TOK + jnp.arange(TOK, dtype=jnp.int32)[None, :]).reshape(-1)
    return position.astype(F32)[:, None] * frequency[None, :]


def turn(block, cosine, sine):
    first, second = block[:, :HALF], block[:, HALF:]
    return jnp.concatenate(
        [first * cosine - second * sine, second * cosine + first * sine], -1
    )


def turn_kernel(x_ref, cos_ref, sin_ref, o_ref):
    o_ref[...] = turn(x_ref[...].astype(F32), cos_ref[...], sin_ref[...]).astype(BF16)


def call_turn(block, cosine, sine):
    return pl.pallas_call(
        turn_kernel,
        out_shape=jax.ShapeDtypeStruct((PAIR, HD), BF16),
        in_specs=[VMEM] * 3,
        out_specs=VMEM,
    )(block, cosine, sine)


def fetch(code, rows, relayed, target, sem):
    for k in range(CHIPS):
        for half in range(CORES):
            @pl.when(code == CORES * k + half)
            def _(k=k, half=half):
                pltpu.make_async_copy(rows[k].at[pl.ds(half * TOK, TOK)], target, sem).start()

        if relayed is not None:
            @pl.when(code == CORES * CHIPS + k)
            def _(k=k):
                pltpu.make_async_copy(relayed[k], target, sem).start()


def await_fetch(rows, target, sem):
    pltpu.make_async_copy(rows[0].at[pl.ds(0, TOK)], target, sem).wait()


def pick_kernel(offset, number, with_relayed, table, *refs):
    rows = refs[:CHIPS]
    relayed = refs[CHIPS : 2 * CHIPS] if with_relayed else None
    o_ref, sem = refs[-2:]
    for i in range(number):
        fetch(table[offset + i], rows, relayed, o_ref.at[pl.ds(i * TOK, TOK)], sem.at[i])
    for i in range(number):
        await_fetch(rows, o_ref.at[pl.ds(i * TOK, TOK)], sem.at[i])


def call_pick(table, rows, relayed, offset, number):
    operands = list(rows) + (list(relayed) if relayed is not None else [])
    return pl.pallas_call(
        functools.partial(pick_kernel, offset, number, relayed is not None),
        out_shape=jax.ShapeDtypeStruct((number * TOK, HD), BF16),
        in_specs=[SMEM] + [ANY] * len(operands),
        out_specs=VMEM,
        scratch_shapes=[pltpu.SemaphoreType.DMA((number,))],
    )(table, *operands)


def attend_kernel(
    table, q_ref, g_ref, cos_ref, sin_ref, other_ref, *refs
):
    rows, relayed = refs[:CHIPS], refs[CHIPS : 2 * CHIPS]
    att_ref, gq_ref, keep_ref, give_ref = refs[2 * CHIPS : 2 * CHIPS + 4]
    mine_ref, q_all, g_all, low_all, score_all, sem = refs[2 * CHIPS + 4 :]
    for i in range(SLOTS):
        fetch(table[i], rows, relayed, mine_ref.at[pl.ds(i * TOK, TOK)], sem.at[i])
    cosine, sine = cos_ref[...], sin_ref[...]
    for h in range(2):
        cols = slice(h * HD, (h + 1) * HD)
        q_all[h * TOK : (h + 1) * TOK, :] = turn(q_ref[:, cols].astype(F32), cosine, sine).astype(BF16)
        g_all[h * TOK : (h + 1) * TOK, :] = g_ref[:, cols]
    for i in range(SLOTS):
        await_fetch(rows, mine_ref.at[pl.ds(i * TOK, TOK)], sem.at[i])
    is_key = table[19] == 0
    mine, other = mine_ref[...], other_ref[...]
    keys = jnp.where(is_key, mine, other)
    vals = jnp.where(is_key, other, mine)
    scaling = HD ** -0.5
    tile = 128
    row_in = lax.broadcasted_iota(jnp.int32, (tile, TOK), 0)
    col_in = lax.broadcasted_iota(jnp.int32, (tile, TOK), 1)
    nt = (((1,), (1,)), ((), ()))
    nn = (((1,), (0,)), ((), ()))
    tn = (((0,), (0,)), ((), ()))
    for t in range(2 * TOK // tile):
        base = (t * tile) % TOK
        rows_here = slice(t * tile, (t + 1) * tile)
        q_tile, g_tile = q_all[rows_here, :], g_all[rows_here, :]
        scores = lax.dot_general(q_tile, keys, nt, preferred_element_type=F32) * scaling
        later = col_in > row_in + base
        seen = [jnp.logical_not(later)]
        for height in range(1, SLOTS):
            here = table[9 + height] > 0
            if height < LEVELS:
                seen.append(jnp.broadcast_to(here, (tile, TOK)))
            else:
                seen.append(jnp.logical_and(later, here))
        visible = jnp.concatenate(seen, 1)
        scores = jnp.where(visible, scores, -1e30)
        top = jnp.max(scores, -1, keepdims=True)
        raw = jnp.where(visible, jnp.exp(scores - top), 0.0)
        probs = raw / jnp.sum(raw, -1, keepdims=True)
        low = probs.astype(BF16)
        low_all[rows_here, :] = low
        att = lax.dot_general(low, vals, nn, preferred_element_type=F32)
        grad_prob = lax.dot_general(g_tile, vals, nt, preferred_element_type=F32)
        delta = jnp.sum(probs * grad_prob, -1, keepdims=True)
        gs = (probs * (grad_prob - delta) * scaling).astype(BF16)
        score_all[rows_here, :] = gs
        gq = lax.dot_general(gs, keys, nn, preferred_element_type=F32)
        h = t * tile // TOK
        toks = slice(base, base + tile)
        att_ref[toks, h * HD : (h + 1) * HD] = att.astype(BF16)
        gq_ref[toks, h * HD : (h + 1) * HD] = turn(
            gq, cos_ref[toks, :], -sin_ref[toks, :]
        ).astype(BF16)
    q2, g2 = q_all[...], g_all[...]
    for i in range(SLOTS):
        cols = slice(i * TOK, (i + 1) * TOK)
        part_key = lax.dot_general(score_all[:, cols], q2, tn, preferred_element_type=F32).astype(BF16)
        part_value = lax.dot_general(low_all[:, cols], g2, tn, preferred_element_type=F32).astype(BF16)
        keep_ref[cols, :] = jnp.where(is_key, part_key, part_value)
        give_ref[cols, :] = jnp.where(is_key, part_value, part_key)


def call_attend(table, query, grad, cosine, sine, other, rows, relayed):
    keys = SLOTS * TOK
    return pl.pallas_call(
        attend_kernel,
        out_shape=(
            jax.ShapeDtypeStruct((TOK, 2 * HD), BF16),
            jax.ShapeDtypeStruct((TOK, 2 * HD), BF16),
            jax.ShapeDtypeStruct((keys, HD), BF16),
            jax.ShapeDtypeStruct((keys, HD), BF16),
        ),
        in_specs=[SMEM] + [VMEM] * 5 + [ANY] * 8,
        out_specs=(VMEM,) * 4,
        scratch_shapes=[
            pltpu.VMEM((keys, HD), BF16),
            pltpu.VMEM((2 * TOK, HD), BF16),
            pltpu.VMEM((2 * TOK, HD), BF16),
            pltpu.VMEM((2 * TOK, keys), BF16),
            pltpu.VMEM((2 * TOK, keys), BF16),
            pltpu.SemaphoreType.DMA((SLOTS,)),
        ],
    )(table, query, grad, cosine, sine, other, *rows, *relayed)


def spread_kernel(table, keep_ref, got_ref, *refs):
    outs, total = refs[:-1], refs[-1]
    total[...] = jnp.zeros_like(total)
    for source, offset in ((keep_ref, 0), (got_ref, SLOTS)):
        for i in range(SLOTS):
            at = pl.ds(pl.multiple_of(table[offset + i] * TOK, TOK), TOK)
            total[at, :] += source[i * TOK : (i + 1) * TOK, :].astype(F32)
    for k in range(CHIPS):
        outs[k][...] = total[k * PAIR : (k + 1) * PAIR, :].astype(outs[k].dtype)
        low = CHIPS * PAIR + k * TOK
        outs[CHIPS + k][...] = total[low : low + TOK, :].astype(BF16)


def call_spread(table, keep, got):
    return pl.pallas_call(
        spread_kernel,
        out_shape=tuple(
            [jax.ShapeDtypeStruct((PAIR, HD), F32)]
            + [jax.ShapeDtypeStruct((PAIR, HD), BF16)] * (CHIPS - 1)
            + [jax.ShapeDtypeStruct((TOK, HD), BF16)] * CHIPS
        ),
        in_specs=[SMEM, VMEM, VMEM],
        out_specs=(VMEM,) * (2 * CHIPS),
        scratch_shapes=[pltpu.VMEM((CHIPS * PAIR + CHIPS * TOK, HD), F32)],
    )(table, keep, got)


def sum_kernel(*refs):
    total = refs[0][...].astype(F32)
    for ref in refs[1:-1]:
        total = total + ref[...].astype(F32)
    refs[-1][...] = total.astype(refs[-1].dtype)


def call_sum(parts, dtype):
    return pl.pallas_call(
        sum_kernel,
        out_shape=jax.ShapeDtypeStruct(parts[0].shape, dtype),
        in_specs=[VMEM] * len(parts),
        out_specs=VMEM,
    )(*parts)


def close_kernel(table, own_ref, *refs):
    backs = refs[:CHIPS]
    cos_ref, sin_ref, o_ref, total = refs[CHIPS:]
    total[...] = own_ref[...]
    for k in range(CHIPS):
        code = table[15 + k]

        @pl.when(code < CORES)
        def _(k=k, code=code):
            at = pl.ds(pl.multiple_of(code * TOK, TOK), TOK)
            total[at, :] += backs[k][...].astype(F32)

    o_ref[...] = turn(total[...], cos_ref[...], -sin_ref[...]).astype(BF16)


def call_close(table, own, backs, cosine, sine):
    return pl.pallas_call(
        close_kernel,
        out_shape=jax.ShapeDtypeStruct((PAIR, HD), BF16),
        in_specs=[SMEM] + [VMEM] * (3 + CHIPS),
        out_specs=VMEM,
        scratch_shapes=[pltpu.VMEM((PAIR, HD), F32)],
    )(table, own, *backs, cosine, sine)


def ring(block, shift):
    return lax.ppermute(block, "chip", [(i, (i + shift) % CHIPS) for i in range(CHIPS)])


def back_in_row(block, shift):
    return lax.ppermute(block, "chip", [(i, i - shift) for i in range(shift, CHIPS)])


def next_row(block, shift):
    rows = lax.axis_size("row")
    return lax.ppermute(
        block, "row", [(i, i + shift) for i in range(rows) if 0 <= i + shift < rows]
    )


def swap(block):
    return lax.ppermute(block, "core", [(0, 1), (1, 0)])


def gather_ring(block):
    near, far = ring(block, 1), ring(block, -1)
    return [block, near, ring(block, 2), far]


def shards(queries, keys, values, grad_attn, parent_gap):
    row, chip, core = (lax.axis_index(name) for name in ("row", "chip", "core"))
    both = lax.all_to_all(
        jnp.concatenate([keys, values], 1), ("core", "head"), split_axis=1, concat_axis=0, tiled=True
    )
    query_in = lax.all_to_all(queries, "head", split_axis=1, concat_axis=0, tiled=True)
    grad_in = lax.all_to_all(grad_attn, "head", split_axis=1, concat_axis=0, tiled=True)
    table, pair_depth = plan(parent_gap, row, chip, core)
    angles = angles_of(pair_depth)
    cosine, sine = jnp.cos(angles), jnp.sin(angles)
    own_cos = lax.dynamic_slice_in_dim(cosine, core * TOK, TOK, 0)
    own_sin = lax.dynamic_slice_in_dim(sine, core * TOK, TOK, 0)
    pair_cos = jnp.where(core == 0, cosine, 1.0)
    pair_sin = jnp.where(core == 0, sine, 0.0)

    both = call_turn(both, pair_cos, pair_sin)
    rows = gather_ring(both)
    relay = next_row(call_pick(table, rows, None, 14, 1), 1)
    relayed = gather_ring(relay)
    other = swap(call_pick(table, rows, relayed, SLOTS, SLOTS))
    attended, grad_query, keep, give = call_attend(
        table, query_in, grad_in, own_cos, own_sin, other, rows, relayed
    )
    spread = call_spread(table, keep, swap(give))
    own, within, stack = spread[0], spread[1:CHIPS], spread[CHIPS:]
    stack_sum = call_sum([stack[0]] + [ring(stack[k], -k) for k in range(1, CHIPS)], BF16)
    back = gather_ring(next_row(stack_sum, -1))
    own = call_sum([own] + [back_in_row(within[k - 1], k) for k in range(1, CHIPS)], F32)
    grad_both = call_close(table, own, back, pair_cos, pair_sin)
    attended_out = lax.all_to_all(attended, "head", split_axis=0, concat_axis=1, tiled=True)
    query_back = lax.all_to_all(grad_query, "head", split_axis=0, concat_axis=1, tiled=True)
    both_back = lax.all_to_all(
        grad_both, ("core", "head"), split_axis=0, concat_axis=1, tiled=True
    )
    half = HEADS * HD
    return attended_out, query_back, both_back[:, :half], both_back[:, half:]


def solution(mesh):
    devices = mesh.devices
    rows = devices.shape[0] // ROW
    split = Mesh(
        devices.reshape(rows, CHIPS, CORES, devices.shape[1]), ("row", "chip", "core", "head")
    )
    spec = P(("row", "chip", "core", "head"), None)
    return jax.shard_map(
        shards,
        mesh=split,
        in_specs=(spec, spec, spec, spec, P()),
        out_specs=(spec, spec, spec, spec),
        check_vma=False,
    )
```

```python
import functools
import math

import jax
import jax.numpy as jnp
from jax import lax
from jax.experimental import pallas as pl
from jax.experimental.pallas import tpu as pltpu
from jax.sharding import Mesh
from jax.sharding import PartitionSpec as P


HD = 256
HALF = HD // 2
TOK = 256
LEVELS = 4
SLOTS = LEVELS + 1
CHIPS = 4
CORES = 2
PAIR = CORES * TOK
KEYS = SLOTS * TOK
ROW = CHIPS * CORES
HEADS = 4
WIDE = 2 * HD
OWN, OTHER, SEEN, GOES, COMES, LAND, CORE = 0, 5, 10, 14, 19, 24, 27
BASE = 10000.0
BF16 = jnp.bfloat16
F32 = jnp.float32

MIB = 1024 * 1024


def room(mib):
    return pltpu.CompilerParams(vmem_limit_bytes=mib * MIB)


ANY = pl.BlockSpec(memory_space=pl.ANY)
VMEM = pl.BlockSpec(memory_space=pltpu.VMEM)
SMEM = pl.BlockSpec(memory_space=pltpu.SMEM)


def plan(parent_gap, row, chip, core):
    count = parent_gap.shape[0]
    ordinal = jnp.arange(count, dtype=jnp.int32)
    levels = jnp.arange(LEVELS, dtype=jnp.int32)
    deeper = (parent_gap == 1).astype(jnp.int32)
    depths = jnp.sum(jnp.where(ordinal[None, :] <= ordinal[:, None], deeper[None, :], 0), 1)
    first = row * ROW
    shard = first + chip * CORES + core
    asked = jnp.stack([shard, shard + 1 - 2 * core, first, first + ROW])
    own_depth = jnp.sum(
        jnp.where(ordinal[None, :] <= asked[:, None], deeper[None, :], 0), 1
    ) + (asked >= count)
    wanted = own_depth[:, None] - 1 - levels[None, :]
    match = (depths[None, None, :] == wanted[:, :, None]) & (
        ordinal[None, None, :] < asked[:, None, None]
    )
    elder = jnp.max(jnp.where(match, ordinal[None, None, :], -1), 2)
    mine, stack, relay = elder[:2], elder[2], elder[3]
    in_row = 2 * (chip - (mine - first) // CORES) + mine % CORES
    before = 2 * CHIPS + 2 * ((mine - first + ROW) // CORES - chip) + mine % CORES
    rank = jnp.sum(jnp.where(mine[:, :, None] == stack[None, None, :], levels, 0), 2)
    source = jnp.where(mine >= first, in_row, before)
    source = jnp.clip(jnp.where(mine >= 0, source, 0), 0, 4 * CHIPS - 1)
    target = jnp.where(mine >= first, in_row, 2 * CHIPS + CHIPS - 1 - rank - chip)
    target = jnp.clip(jnp.where(mine >= 0, target, 0), 0, 3 * CHIPS - 1)
    own = jnp.stack([core, 1 - core])[:, None]
    source = jnp.concatenate([own, source], 1).reshape(-1)
    target = jnp.concatenate([own, target], 1).reshape(-1)
    held = jnp.stack([CHIPS - 1 - chip, CHIPS - chip, jnp.where(chip == 2, CHIPS - 1, CHIPS)])
    node = jnp.sum(jnp.where(held[:, None] == levels[None, :], relay[None, :], 0), 1)
    here = (held < LEVELS) & (node >= first) & ((node - first) // CORES == chip)
    land = jnp.where(here, node % CORES, CORES)
    table = jnp.concatenate(
        [source, (elder[0] >= 0).astype(jnp.int32), target, land, core[None]]
    ).astype(jnp.int32)
    slot_depth = own_depth[0] - jnp.arange(SLOTS, dtype=jnp.int32)
    pair_depth = jnp.where(core == 0, own_depth[:2], own_depth[1::-1])
    return table, slot_depth, pair_depth


def angles_of(depth):
    frequency = jnp.exp(jnp.arange(HALF, dtype=F32) * (-2.0 * math.log(BASE) / HD))
    position = (depth[:, None] * TOK + jnp.arange(TOK, dtype=jnp.int32)[None, :]).reshape(-1)
    return position.astype(F32)[:, None] * frequency[None, :]


def turn(block, cosine, sine):
    first, second = block[:, :HALF], block[:, HALF:]
    return jnp.concatenate(
        [first * cosine - second * sine, second * cosine + first * sine], -1
    )


def fetch(code, sources, target, sem):
    for k, ref in enumerate(sources):
        for half in range(CORES):

            @pl.when(code == CORES * k + half)
            def _(ref=ref, half=half):
                pltpu.make_async_copy(ref.at[pl.ds(half * TOK, TOK)], target, sem).start()


def await_fetch(sources, target, sem):
    pltpu.make_async_copy(sources[0].at[pl.ds(0, TOK)], target, sem).wait()


def pick_kernel(table, *refs):
    sources, (o_ref, sem) = refs[:-2], refs[-2:]
    for i in range(SLOTS):
        fetch(table[OTHER + i], sources, o_ref.at[pl.ds(i * TOK, TOK)], sem.at[i])
    for i in range(SLOTS):
        await_fetch(sources, o_ref.at[pl.ds(i * TOK, TOK)], sem.at[i])


def call_pick(table, sources):
    return pl.pallas_call(
        pick_kernel,
        compiler_params=room(4),
        out_shape=jax.ShapeDtypeStruct((KEYS, HD), BF16),
        in_specs=[SMEM] + [ANY] * len(sources),
        out_specs=VMEM,
        scratch_shapes=[pltpu.SemaphoreType.DMA((SLOTS,))],
    )(table, *sources)


NT = (((1,), (1,)), ((), ()))
NN = (((1,), (0,)), ((), ()))
TN = (((0,), (0,)), ((), ()))


def dot(a, b, dims):
    return lax.dot_general(a, b, dims, preferred_element_type=F32)


def attend_kernel(table, qg_ref, cos_ref, sin_ref, other_ref, *refs):
    sources = refs[: 2 * CHIPS]
    out_ref, keep_ref, give_ref = refs[2 * CHIPS : 2 * CHIPS + 3]
    mine_ref, keys, vals, q_all, low_all, score_all, sem = refs[2 * CHIPS + 3 :]
    for i in range(SLOTS):
        fetch(table[OWN + i], sources, mine_ref.at[pl.ds(i * TOK, TOK)], sem.at[i])
    for h in range(2):
        q_all[h * TOK : (h + 1) * TOK, :] = turn(
            qg_ref[:, h * HD : (h + 1) * HD].astype(F32), cos_ref[:TOK, :], sin_ref[:TOK, :]
        ).astype(BF16)
    is_key = table[CORE] == 0
    for i in range(SLOTS):
        here = slice(i * TOK, (i + 1) * TOK)
        await_fetch(sources, mine_ref.at[pl.ds(i * TOK, TOK)], sem.at[i])
        mine, other = mine_ref[here, :], other_ref[here, :]
        keys[here, :] = turn(
            jnp.where(is_key, mine, other).astype(F32), cos_ref[here, :], sin_ref[here, :]
        ).astype(BF16)
        vals[here, :] = jnp.where(is_key, other, mine)
    scaling = HD**-0.5
    earlier = lax.broadcasted_iota(jnp.int32, (TOK, TOK), 1) <= lax.broadcasted_iota(
        jnp.int32, (TOK, TOK), 0
    )
    last = SLOTS - 1
    block = lambda ref, i: ref[i * TOK : (i + 1) * TOK, :]
    for h in range(2):
        rows = slice(h * TOK, (h + 1) * TOK)
        q, g = q_all[rows, :], qg_ref[:, WIDE + h * HD : WIDE + (h + 1) * HD]

        def joint(a, which, fill):
            parts = [dot(a, block(which, i), NT) for i in range(SLOTS)]
            if fill is None:
                return [jnp.where(earlier, parts[0], parts[last])] + parts[1:last]
            parts = [parts[0] * scaling] + [
                jnp.where(table[SEEN + i - 1] > 0, parts[i] * scaling, fill)
                for i in range(1, SLOTS)
            ]
            return [jnp.where(earlier, parts[0], parts[last])] + parts[1:last]

        scores = joint(q, keys, -1e30)
        top = functools.reduce(jnp.maximum, scores)
        top = jnp.max(top, -1, keepdims=True)
        raw = [jnp.exp(s - top) for s in scores]
        share = 1.0 / jnp.sum(functools.reduce(jnp.add, raw), -1, keepdims=True)
        probs = [r * share for r in raw]
        grads = joint(g, vals, None)
        delta = functools.reduce(jnp.add, [p * d for p, d in zip(probs, grads)])
        delta = jnp.sum(delta, -1, keepdims=True)
        for ref, parts in (
            (low_all, probs),
            (score_all, [p * (d - delta) * scaling for p, d in zip(probs, grads)]),
        ):
            ref[rows, :TOK] = jnp.where(earlier, parts[0], 0.0).astype(BF16)
            ref[rows, last * TOK :] = jnp.where(earlier, 0.0, parts[0]).astype(BF16)
            for i in range(1, last):
                ref[rows, i * TOK : (i + 1) * TOK] = parts[i].astype(BF16)
        out_ref[:, h * HD : (h + 1) * HD] = dot(low_all[rows, :], vals[...], NN).astype(BF16)
        out_ref[:, WIDE + h * HD : WIDE + (h + 1) * HD] = turn(
            dot(score_all[rows, :], keys[...], NN), cos_ref[:TOK, :], -sin_ref[:TOK, :]
        ).astype(BF16)
    for i in range(SLOTS):
        cols = slice(i * TOK, (i + 1) * TOK)
        part_key = dot(score_all[:, cols], q_all[...], TN)
        part_value = dot(low_all[:TOK, cols], qg_ref[:, WIDE : WIDE + HD], TN) + dot(
            low_all[TOK:, cols], qg_ref[:, WIDE + HD :], TN
        )
        keep_ref[cols, :] = jnp.where(is_key, part_key, part_value).astype(BF16)
        give_ref[cols, :] = jnp.where(is_key, part_value, part_key).astype(BF16)


def call_attend(table, query_grad, cosine, sine, other, sources):
    return pl.pallas_call(
        attend_kernel,
        compiler_params=room(24),
        out_shape=(
            jax.ShapeDtypeStruct((TOK, 2 * WIDE), BF16),
            jax.ShapeDtypeStruct((KEYS, HD), BF16),
            jax.ShapeDtypeStruct((KEYS, HD), BF16),
        ),
        in_specs=[SMEM] + [VMEM] * 4 + [ANY] * len(sources),
        out_specs=(VMEM,) * 3,
        scratch_shapes=[
            pltpu.VMEM((KEYS, HD), BF16),
            pltpu.VMEM((KEYS, HD), BF16),
            pltpu.VMEM((KEYS, HD), BF16),
            pltpu.VMEM((2 * TOK, HD), BF16),
            pltpu.VMEM((2 * TOK, KEYS), BF16),
            pltpu.VMEM((2 * TOK, KEYS), BF16),
            pltpu.SemaphoreType.DMA((SLOTS,)),
        ],
    )(table, query_grad, cosine, sine, other, *sources)


def spread_kernel(table, keep_ref, got_ref, *refs):
    outs, total = refs[:-1], refs[-1]
    total[...] = jnp.zeros_like(total)
    for source, offset in ((keep_ref, GOES), (got_ref, COMES)):
        for i in range(SLOTS):
            at = pl.ds(pl.multiple_of(table[offset + i] * TOK, TOK), TOK)
            total[at, :] += source[i * TOK : (i + 1) * TOK, :].astype(F32)
    for k in range(CHIPS):
        outs[k][...] = total[k * PAIR : (k + 1) * PAIR, :].astype(outs[k].dtype)
        low = CHIPS * PAIR + k * TOK
        outs[CHIPS + k][...] = total[low : low + TOK, :].astype(BF16)


def call_spread(table, keep, got):
    return pl.pallas_call(
        spread_kernel,
        compiler_params=room(12),
        out_shape=tuple(
            [jax.ShapeDtypeStruct((PAIR, HD), F32)]
            + [jax.ShapeDtypeStruct((PAIR, HD), BF16)] * (CHIPS - 1)
            + [jax.ShapeDtypeStruct((TOK, HD), BF16)] * CHIPS
        ),
        in_specs=[SMEM, VMEM, VMEM],
        out_specs=(VMEM,) * (2 * CHIPS),
        scratch_shapes=[pltpu.VMEM((CHIPS * PAIR + CHIPS * TOK, HD), F32)],
    )(table, keep, got)


def sum_kernel(*refs):
    total = refs[0][...].astype(F32)
    for ref in refs[1:-1]:
        total = total + ref[...].astype(F32)
    refs[-1][...] = total.astype(refs[-1].dtype)


def call_sum(parts, dtype):
    return pl.pallas_call(
        sum_kernel,
        compiler_params=room(6),
        out_shape=jax.ShapeDtypeStruct(parts[0].shape, dtype),
        in_specs=[VMEM] * len(parts),
        out_specs=VMEM,
    )(*parts)


def close_kernel(table, own_ref, *refs):
    backs = refs[:-4]
    cos_ref, sin_ref, o_ref, total = refs[-4:]
    total[...] = own_ref[...]
    for k, back in enumerate(backs):
        code = table[LAND + k]

        @pl.when(code < CORES)
        def _(back=back, code=code):
            at = pl.ds(pl.multiple_of(code * TOK, TOK), TOK)
            total[at, :] += back[...].astype(F32)

    is_key = table[CORE] == 0

    @pl.when(is_key)
    def _():
        o_ref[...] = turn(total[...], cos_ref[...], -sin_ref[...]).astype(BF16)

    @pl.when(jnp.logical_not(is_key))
    def _():
        o_ref[...] = total[...].astype(BF16)


def call_close(table, own, backs, cosine, sine):
    return pl.pallas_call(
        close_kernel,
        compiler_params=room(8),
        out_shape=jax.ShapeDtypeStruct((PAIR, HD), BF16),
        in_specs=[SMEM] + [VMEM] * (3 + len(backs)),
        out_specs=VMEM,
        scratch_shapes=[pltpu.VMEM((PAIR, HD), F32)],
    )(table, own, *backs, cosine, sine)


def along(block, shift, starts=range(CHIPS)):
    return lax.ppermute(
        block, "chip", [(i, i + shift) for i in starts if 0 <= i + shift < CHIPS]
    )


def next_row(block, shift):
    rows = lax.axis_size("row")
    return lax.ppermute(
        block, "row", [(i, i + shift) for i in range(rows) if 0 <= i + shift < rows]
    )


def swap(block):
    return lax.ppermute(block, "core", [(0, 1), (1, 0)])


def shards(queries, keys, values, grad_attn, parent_gap):
    row, chip, core = (lax.axis_index(name) for name in ("row", "chip", "core"))
    tokens = queries.shape[0]
    both = lax.all_to_all(
        jnp.concatenate([keys, values], 1),
        ("core", "head"),
        split_axis=1,
        concat_axis=0,
        tiled=True,
    )
    table, slot_depth, pair_depth = plan(parent_gap, row, chip, core)
    slot_angles, pair_angles = angles_of(slot_depth), angles_of(pair_depth)
    slot_cos, slot_sin = jnp.cos(slot_angles), jnp.sin(slot_angles)
    pair_cos, pair_sin = jnp.cos(pair_angles), jnp.sin(pair_angles)
    table, slot_cos, slot_sin, pair_cos, pair_sin = lax.optimization_barrier(
        (table, slot_cos, slot_sin, pair_cos, pair_sin)
    )

    relay = next_row(both, 1)
    sources = [both] + [along(both, k) for k in (1, 2, 3)]
    query_grad = jnp.concatenate(
        [queries.reshape(tokens, HEADS, WIDE), grad_attn.reshape(tokens, HEADS, WIDE)], 2
    ).reshape(tokens, HEADS * 2 * WIDE)
    query_grad = lax.all_to_all(query_grad, "head", split_axis=1, concat_axis=0, tiled=True)
    sources += [relay] + [along(relay, -k) for k in (1, 2, 3)]
    other = swap(call_pick(table, sources))
    out, keep, give = call_attend(table, query_grad, slot_cos, slot_sin, other, sources)
    got = swap(give)
    out = lax.all_to_all(out, "head", split_axis=0, concat_axis=1, tiled=True)
    out = out.reshape(tokens, HEADS, 2, WIDE)
    attended = out[:, :, 0].reshape(tokens, HEADS * WIDE)
    grad_query = out[:, :, 1].reshape(tokens, HEADS * WIDE)
    spread = call_spread(table, keep, got)
    own, within, stack = spread[0], spread[1:CHIPS], spread[CHIPS:]
    stack_sum = call_sum([stack[0]] + [along(stack[k], k) for k in (1, 2, 3)], BF16)
    back = next_row(stack_sum, -1)
    own = call_sum([own] + [along(within[k - 1], -k) for k in (1, 2, 3)], F32)
    backs = [back, along(back, 1), along(back, 2, (0,))]
    grad_both = call_close(table, own, backs, pair_cos, pair_sin)
    grad_both = lax.all_to_all(grad_both, ("core", "head"), split_axis=0, concat_axis=1, tiled=True)
    half = HEADS * HD
    return attended, grad_query, grad_both[:, :half], grad_both[:, half:]


def solution(mesh):
    devices = mesh.devices
    rows = devices.shape[0] // ROW
    split = Mesh(
        devices.reshape(rows, CHIPS, CORES, devices.shape[1]), ("row", "chip", "core", "head")
    )
    spec = P(("row", "chip", "core", "head"), None)

    return jax.shard_map(
        shards,
        mesh=split,
        in_specs=(spec, spec, spec, spec, P()),
        out_specs=(spec, spec, spec, spec),
        check_vma=False,
    )
```

```python
import functools
import math

import jax
import jax.numpy as jnp
from jax import lax
from jax.experimental import pallas as pl
from jax.experimental.pallas import tpu as pltpu
from jax.sharding import Mesh
from jax.sharding import PartitionSpec as P


HD = 256
HALF = HD // 2
TOK = 256
LEVELS = 4
SLOTS = LEVELS + 1
CHIPS = 4
CORES = 2
PAIR = CORES * TOK
KEYS = SLOTS * TOK
ROW = CHIPS * CORES
HEADS = 4
WIDE = 2 * HD
OWN, OTHER, SEEN, SEND, LAND, CORE = 0, 5, 10, 14, 15, 18
BASE = 10000.0
BF16 = jnp.bfloat16
F32 = jnp.float32

MIB = 1024 * 1024


def room(mib):
    return pltpu.CompilerParams(vmem_limit_bytes=mib * MIB)


ANY = pl.BlockSpec(memory_space=pl.ANY)
VMEM = pl.BlockSpec(memory_space=pltpu.VMEM)
SMEM = pl.BlockSpec(memory_space=pltpu.SMEM)


def plan(parent_gap, row, chip, core):
    count = parent_gap.shape[0]
    ordinal = jnp.arange(count, dtype=jnp.int32)
    levels = jnp.arange(LEVELS, dtype=jnp.int32)
    deeper = (parent_gap == 1).astype(jnp.int32)
    depths = jnp.sum(jnp.where(ordinal[None, :] <= ordinal[:, None], deeper[None, :], 0), 1)
    first = row * ROW
    shard = first + chip * CORES + core
    asked = jnp.stack([shard, shard + 1 - 2 * core, first, first + ROW])
    own_depth = jnp.sum(
        jnp.where(ordinal[None, :] <= asked[:, None], deeper[None, :], 0), 1
    ) + (asked >= count)
    wanted = own_depth[:, None] - 1 - levels[None, :]
    match = (depths[None, None, :] == wanted[:, :, None]) & (
        ordinal[None, None, :] < asked[:, None, None]
    )
    elder = jnp.max(jnp.where(match, ordinal[None, None, :], -1), 2)
    mine, stack, relay = elder[:2], elder[2], elder[3]
    in_row = 2 * (chip - (mine - first) // CORES) + mine % CORES
    holder = CHIPS - 1 - jnp.sum(
        jnp.where(mine[:, :, None] == stack[None, None, :], levels, 0), 2
    )
    code = jnp.where(mine >= first, in_row, 2 * CHIPS + holder - chip)
    code = jnp.clip(jnp.where(mine >= 0, code, 0), 0, 3 * CHIPS - 1)
    code = jnp.concatenate([jnp.stack([core, 1 - core])[:, None], code], 1).reshape(-1)
    held = jnp.sum(jnp.where(levels == CHIPS - 1 - chip, relay, 0))
    far = (held - first) // CORES - chip
    send = jnp.clip(2 * far + held % CORES, 0, 2 * CHIPS - 3)
    held = jnp.stack([CHIPS - 1 - chip, CHIPS - chip, jnp.where(chip == 2, CHIPS - 1, CHIPS)])
    node = jnp.sum(jnp.where(held[:, None] == levels[None, :], relay[None, :], 0), 1)
    here = (held < LEVELS) & (node >= first) & ((node - first) // CORES == chip)
    land = jnp.where(here, node % CORES, CORES)
    table = jnp.concatenate(
        [code, (elder[0] >= 0).astype(jnp.int32), send[None], land, core[None]]
    ).astype(jnp.int32)
    slot_depth = own_depth[0] - jnp.arange(SLOTS, dtype=jnp.int32)
    pair_depth = jnp.where(core == 0, own_depth[:2], own_depth[1::-1])
    return table, slot_depth, pair_depth


def angles_of(depth):
    frequency = jnp.exp(jnp.arange(HALF, dtype=F32) * (-2.0 * math.log(BASE) / HD))
    position = (depth[:, None] * TOK + jnp.arange(TOK, dtype=jnp.int32)[None, :]).reshape(-1)
    return position.astype(F32)[:, None] * frequency[None, :]


def turn(block, cosine, sine):
    first, second = block[:, :HALF], block[:, HALF:]
    return jnp.concatenate(
        [first * cosine - second * sine, second * cosine + first * sine], -1
    )


def fetch(code, sources, target, sem):
    at = 0
    for ref in sources:
        for half in range(ref.shape[0] // TOK):

            @pl.when(code == at)
            def _(ref=ref, half=half):
                pltpu.make_async_copy(ref.at[pl.ds(half * TOK, TOK)], target, sem).start()

            at += 1


def await_fetch(sources, target, sem):
    pltpu.make_async_copy(sources[0].at[pl.ds(0, TOK)], target, sem).wait()


def part(ref, i):
    return ref.at[pl.ds(i * TOK, TOK)]


def pick_kernel(offset, number, table, *refs):
    sources, (o_ref, sem) = refs[:-2], refs[-2:]
    for i in range(number):
        fetch(table[offset + i], sources, part(o_ref, i), sem.at[i])
    for i in range(number):
        await_fetch(sources, part(o_ref, i), sem.at[i])


def call_pick(table, sources, offset, number):
    return pl.pallas_call(
        functools.partial(pick_kernel, offset, number),
        compiler_params=room(4),
        out_shape=jax.ShapeDtypeStruct((number * TOK, HD), BF16),
        in_specs=[SMEM] + [ANY] * len(sources),
        out_specs=VMEM,
        scratch_shapes=[pltpu.SemaphoreType.DMA((number,))],
    )(table, *sources)


NT = (((1,), (1,)), ((), ()))
NN = (((1,), (0,)), ((), ()))
TN = (((0,), (0,)), ((), ()))


def dot(a, b, dims):
    return lax.dot_general(a, b, dims, preferred_element_type=F32)


def attend_kernel(table, qg_hbm, cos_hbm, sin_hbm, other_hbm, *refs):
    sources = refs[: 2 * CHIPS]
    out_hbm, keep_hbm, give_hbm = refs[2 * CHIPS : 2 * CHIPS + 3]
    (qg_ref, cos_ref, sin_ref, mine_ref, other_ref, keys, vals, q_all, low_all, score_all) = refs[
        2 * CHIPS + 3 : 2 * CHIPS + 13
    ]
    out_ref, keep_ref, give_ref, sem, in_sem, out_sem = refs[2 * CHIPS + 13 :]
    whole_in = [
        pltpu.make_async_copy(src, dst, in_sem.at[i])
        for i, (src, dst) in enumerate(
            ((qg_hbm, qg_ref), (cos_hbm, cos_ref), (sin_hbm, sin_ref))
        )
    ]
    other_in = [
        pltpu.make_async_copy(part(other_hbm, i), part(other_ref, i), sem.at[SLOTS + i])
        for i in range(SLOTS)
    ]
    for copy in whole_in:
        copy.start()
    for i in range(SLOTS):
        fetch(table[OWN + i], sources, part(mine_ref, i), sem.at[i])
        other_in[i].start()
    for copy in whole_in:
        copy.wait()
    for h in range(2):
        q_all[h * TOK : (h + 1) * TOK, :] = turn(
            qg_ref[:, h * HD : (h + 1) * HD].astype(F32), cos_ref[:TOK, :], sin_ref[:TOK, :]
        ).astype(BF16)
    is_key = table[CORE] == 0
    for i in range(SLOTS):
        here = slice(i * TOK, (i + 1) * TOK)
        await_fetch(sources, part(mine_ref, i), sem.at[i])
        other_in[i].wait()
        mine, other = mine_ref[here, :], other_ref[here, :]
        keys[here, :] = turn(
            jnp.where(is_key, mine, other).astype(F32), cos_ref[here, :], sin_ref[here, :]
        ).astype(BF16)
        vals[here, :] = jnp.where(is_key, other, mine)
    scaling = HD**-0.5
    earlier = lax.broadcasted_iota(jnp.int32, (TOK, TOK), 1) <= lax.broadcasted_iota(
        jnp.int32, (TOK, TOK), 0
    )
    last = SLOTS - 1
    block = lambda ref, i: ref[i * TOK : (i + 1) * TOK, :]
    for h in range(2):
        rows = slice(h * TOK, (h + 1) * TOK)
        q, g = q_all[rows, :], qg_ref[:, WIDE + h * HD : WIDE + (h + 1) * HD]

        def joint(a, which, fill):
            parts = [dot(a, block(which, i), NT) for i in range(SLOTS)]
            if fill is None:
                return [jnp.where(earlier, parts[0], parts[last])] + parts[1:last]
            parts = [parts[0] * scaling] + [
                jnp.where(table[SEEN + i - 1] > 0, parts[i] * scaling, fill)
                for i in range(1, SLOTS)
            ]
            return [jnp.where(earlier, parts[0], parts[last])] + parts[1:last]

        scores = joint(q, keys, -1e30)
        top = functools.reduce(jnp.maximum, scores)
        top = jnp.max(top, -1, keepdims=True)
        raw = [jnp.exp(s - top) for s in scores]
        share = 1.0 / jnp.sum(functools.reduce(jnp.add, raw), -1, keepdims=True)
        probs = [r * share for r in raw]
        grads = joint(g, vals, None)
        delta = functools.reduce(jnp.add, [p * d for p, d in zip(probs, grads)])
        delta = jnp.sum(delta, -1, keepdims=True)
        for ref, parts in (
            (low_all, probs),
            (score_all, [p * (d - delta) * scaling for p, d in zip(probs, grads)]),
        ):
            ref[rows, :TOK] = jnp.where(earlier, parts[0], 0.0).astype(BF16)
            ref[rows, last * TOK :] = jnp.where(earlier, 0.0, parts[0]).astype(BF16)
            for i in range(1, last):
                ref[rows, i * TOK : (i + 1) * TOK] = parts[i].astype(BF16)
        out_ref[:, h * HD : (h + 1) * HD] = dot(low_all[rows, :], vals[...], NN).astype(BF16)
        out_ref[:, WIDE + h * HD : WIDE + (h + 1) * HD] = turn(
            dot(score_all[rows, :], keys[...], NN), cos_ref[:TOK, :], -sin_ref[:TOK, :]
        ).astype(BF16)
    outgoing = [pltpu.make_async_copy(out_ref, out_hbm, out_sem.at[0])]
    outgoing[0].start()
    for i in range(SLOTS):
        cols = slice(i * TOK, (i + 1) * TOK)
        part_key = dot(score_all[:, cols], q_all[...], TN)
        part_value = dot(low_all[:TOK, cols], qg_ref[:, WIDE : WIDE + HD], TN) + dot(
            low_all[TOK:, cols], qg_ref[:, WIDE + HD :], TN
        )
        keep_ref[cols, :] = jnp.where(is_key, part_key, part_value).astype(BF16)
        give_ref[cols, :] = jnp.where(is_key, part_value, part_key).astype(BF16)
        for k, (src, dst) in enumerate(((give_ref, give_hbm), (keep_ref, keep_hbm))):
            outgoing.append(
                pltpu.make_async_copy(part(src, i), part(dst, i), out_sem.at[1 + 2 * i + k])
            )
            outgoing[-1].start()
    for copy in outgoing:
        copy.wait()


def call_attend(table, query_grad, cosine, sine, other, sources):
    return pl.pallas_call(
        attend_kernel,
        out_shape=(
            jax.ShapeDtypeStruct((TOK, 2 * WIDE), BF16),
            jax.ShapeDtypeStruct((KEYS, HD), BF16),
            jax.ShapeDtypeStruct((KEYS, HD), BF16),
        ),
        in_specs=[SMEM] + [ANY] * (4 + len(sources)),
        out_specs=(ANY,) * 3,
        scratch_shapes=[
            pltpu.VMEM((TOK, 2 * WIDE), BF16),
            pltpu.VMEM((KEYS, HALF), F32),
            pltpu.VMEM((KEYS, HALF), F32),
            pltpu.VMEM((KEYS, HD), BF16),
            pltpu.VMEM((KEYS, HD), BF16),
            pltpu.VMEM((KEYS, HD), BF16),
            pltpu.VMEM((KEYS, HD), BF16),
            pltpu.VMEM((2 * TOK, HD), BF16),
            pltpu.VMEM((2 * TOK, KEYS), BF16),
            pltpu.VMEM((2 * TOK, KEYS), BF16),
            pltpu.VMEM((TOK, 2 * WIDE), BF16),
            pltpu.VMEM((KEYS, HD), BF16),
            pltpu.VMEM((KEYS, HD), BF16),
            pltpu.SemaphoreType.DMA((2 * SLOTS,)),
            pltpu.SemaphoreType.DMA((3,)),
            pltpu.SemaphoreType.DMA((1 + 2 * SLOTS,)),
        ],
    )(table, query_grad, cosine, sine, other, *sources)


def spread_kernel(table, keep_hbm, got_hbm, *refs):
    outs, (total, terms, own_ref, within_ref, stack_ref, sem, out_sem) = refs[:-7], refs[-7:]
    copies = [
        [
            pltpu.make_async_copy(part(src, i), part(terms.at[k], i), sem.at[k, i])
            for i in range(SLOTS)
        ]
        for k, src in enumerate((keep_hbm, got_hbm))
    ]
    for group in copies:
        for copy in group:
            copy.start()
    total[...] = jnp.zeros_like(total)
    for k, offset in enumerate((OWN, OTHER)):
        source = terms.at[k]
        for i in range(SLOTS):
            copies[k][i].wait()
            at = pl.ds(pl.multiple_of(table[offset + i] * TOK, TOK), TOK)
            total[at, :] += source[i * TOK : (i + 1) * TOK, :].astype(F32)
    outgoing = []

    def leave(src, dst):
        outgoing.append(pltpu.make_async_copy(src, dst, out_sem.at[len(outgoing)]))
        outgoing[-1].start()

    for k in range(CHIPS):
        low = CHIPS * PAIR + k * TOK
        stack_ref[k] = total[low : low + TOK, :].astype(BF16)
        leave(stack_ref.at[k], outs[CHIPS + k])
    for k in range(1, CHIPS):
        within_ref[k - 1] = total[k * PAIR : (k + 1) * PAIR, :].astype(BF16)
        leave(within_ref.at[k - 1], outs[k])
    own_ref[...] = total[:PAIR, :]
    leave(own_ref, outs[0])
    for copy in outgoing:
        copy.wait()


def call_spread(table, keep, got):
    return pl.pallas_call(
        spread_kernel,
        compiler_params=room(12),
        out_shape=tuple(
            [jax.ShapeDtypeStruct((PAIR, HD), F32)]
            + [jax.ShapeDtypeStruct((PAIR, HD), BF16)] * (CHIPS - 1)
            + [jax.ShapeDtypeStruct((TOK, HD), BF16)] * CHIPS
        ),
        in_specs=[SMEM, ANY, ANY],
        out_specs=(ANY,) * (2 * CHIPS),
        scratch_shapes=[
            pltpu.VMEM((CHIPS * PAIR + CHIPS * TOK, HD), F32),
            pltpu.VMEM((CORES, KEYS, HD), BF16),
            pltpu.VMEM((PAIR, HD), F32),
            pltpu.VMEM((CHIPS - 1, PAIR, HD), BF16),
            pltpu.VMEM((CHIPS, TOK, HD), BF16),
            pltpu.SemaphoreType.DMA((CORES, SLOTS)),
            pltpu.SemaphoreType.DMA((2 * CHIPS,)),
        ],
    )(table, keep, got)


def sum_kernel(*refs):
    total = refs[0][...].astype(F32)
    for ref in refs[1:-1]:
        total = total + ref[...].astype(F32)
    refs[-1][...] = total.astype(refs[-1].dtype)


def call_sum(parts, dtype):
    return pl.pallas_call(
        sum_kernel,
        compiler_params=room(6),
        out_shape=jax.ShapeDtypeStruct(parts[0].shape, dtype),
        in_specs=[VMEM] * len(parts),
        out_specs=VMEM,
    )(*parts)


def close_kernel(table, own_ref, *refs):
    backs = refs[:-4]
    cos_ref, sin_ref, o_ref, total = refs[-4:]
    total[...] = own_ref[...]
    for k, back in enumerate(backs):
        code = table[LAND + k]

        @pl.when(code < CORES)
        def _(back=back, code=code):
            at = pl.ds(pl.multiple_of(code * TOK, TOK), TOK)
            total[at, :] += back[...].astype(F32)

    is_key = table[CORE] == 0

    @pl.when(is_key)
    def _():
        o_ref[...] = turn(total[...], cos_ref[...], -sin_ref[...]).astype(BF16)

    @pl.when(jnp.logical_not(is_key))
    def _():
        o_ref[...] = total[...].astype(BF16)


def call_close(table, own, backs, cosine, sine):
    return pl.pallas_call(
        close_kernel,
        compiler_params=room(8),
        out_shape=jax.ShapeDtypeStruct((PAIR, HD), BF16),
        in_specs=[SMEM] + [VMEM] * (3 + len(backs)),
        out_specs=VMEM,
        scratch_shapes=[pltpu.VMEM((PAIR, HD), F32)],
    )(table, own, *backs, cosine, sine)


def along(block, shift, starts=range(CHIPS)):
    return lax.ppermute(
        block, "chip", [(i, i + shift) for i in starts if 0 <= i + shift < CHIPS]
    )


def next_row(block, shift):
    rows = lax.axis_size("row")
    return lax.ppermute(
        block, "row", [(i, i + shift) for i in range(rows) if 0 <= i + shift < rows]
    )


def swap(block):
    return lax.ppermute(block, "core", [(0, 1), (1, 0)])


def shards(queries, keys, values, grad_attn, parent_gap):
    row, chip, core = (lax.axis_index(name) for name in ("row", "chip", "core"))
    tokens = queries.shape[0]
    both = lax.all_to_all(
        jnp.concatenate([keys, values], 1),
        ("core", "head"),
        split_axis=1,
        concat_axis=0,
        tiled=True,
    )
    table, slot_depth, pair_depth = plan(parent_gap, row, chip, core)
    slot_angles, pair_angles = angles_of(slot_depth), angles_of(pair_depth)
    slot_cos, slot_sin = jnp.cos(slot_angles), jnp.sin(slot_angles)
    pair_cos, pair_sin = jnp.cos(pair_angles), jnp.sin(pair_angles)
    table, slot_cos, slot_sin, pair_cos, pair_sin = lax.optimization_barrier(
        (table, slot_cos, slot_sin, pair_cos, pair_sin)
    )

    pairs = [both, along(both, -1), along(both, -2, (2,))]
    relay = next_row(call_pick(table, pairs, SEND, 1), 1)
    sources = [both] + [along(both, k) for k in (1, 2, 3)]
    query_grad = jnp.concatenate(
        [queries.reshape(tokens, HEADS, WIDE), grad_attn.reshape(tokens, HEADS, WIDE)], 2
    ).reshape(tokens, HEADS * 2 * WIDE)
    query_grad = lax.all_to_all(query_grad, "head", split_axis=1, concat_axis=0, tiled=True)
    sources += [relay] + [along(relay, -k) for k in (1, 2, 3)]
    other = swap(call_pick(table, sources, OTHER, SLOTS))
    out, keep, give = call_attend(table, query_grad, slot_cos, slot_sin, other, sources)
    got = swap(give)
    out = lax.all_to_all(out, "head", split_axis=0, concat_axis=1, tiled=True)
    spread = call_spread(table, keep, got)
    own, within, stack = spread[0], spread[1:CHIPS], spread[CHIPS:]
    stack_sum = call_sum([stack[0]] + [along(stack[k], k) for k in (1, 2, 3)], BF16)
    back = next_row(stack_sum, -1)
    own = call_sum([own] + [along(within[k - 1], -k) for k in (1, 2, 3)], F32)
    backs = [back, along(back, 1), along(back, 2, (0,))]
    grad_both = call_close(table, own, backs, pair_cos, pair_sin)
    grad_both, out = lax.optimization_barrier((grad_both, out))
    grad_both = lax.all_to_all(grad_both, ("core", "head"), split_axis=0, concat_axis=1, tiled=True)
    out = out.reshape(tokens, HEADS, 2, WIDE)
    attended = out[:, :, 0].reshape(tokens, HEADS * WIDE)
    grad_query = out[:, :, 1].reshape(tokens, HEADS * WIDE)
    half = HEADS * HD
    return attended, grad_query, grad_both[:, :half], grad_both[:, half:]


def solution(mesh):
    devices = mesh.devices
    rows = devices.shape[0] // ROW
    split = Mesh(
        devices.reshape(rows, CHIPS, CORES, devices.shape[1]), ("row", "chip", "core", "head")
    )
    spec = P(("row", "chip", "core", "head"), None)

    return jax.shard_map(
        shards,
        mesh=split,
        in_specs=(spec, spec, spec, spec, P()),
        out_specs=(spec, spec, spec, spec),
        check_vma=False,
    )
```

```python
import functools
import math

import jax
import jax.numpy as jnp
from jax import lax
from jax.experimental import pallas as pl
from jax.experimental.pallas import tpu as pltpu
from jax.sharding import Mesh
from jax.sharding import PartitionSpec as P


HD = 256
HALF = HD // 2
TOK = 256
LEVELS = 4
SLOTS = LEVELS + 1
CHIPS = 4
CORES = 2
PAIR = CORES * TOK
KEYS = SLOTS * TOK
ROW = CHIPS * CORES
HEADS = 4
WIDE = 2 * HD
OWN, OTHER, SEEN, SEND, LAND, CORE = 0, 5, 10, 14, 15, 18
BASE = 10000.0
BF16 = jnp.bfloat16
F32 = jnp.float32

MIB = 1024 * 1024


def room(mib):
    return pltpu.CompilerParams(vmem_limit_bytes=mib * MIB)


ANY = pl.BlockSpec(memory_space=pl.ANY)
VMEM = pl.BlockSpec(memory_space=pltpu.VMEM)
SMEM = pl.BlockSpec(memory_space=pltpu.SMEM)


def plan(parent_gap, row, chip, core):
    count = parent_gap.shape[0]
    ordinal = jnp.arange(count, dtype=jnp.int32)
    levels = jnp.arange(LEVELS, dtype=jnp.int32)
    deeper = (parent_gap == 1).astype(jnp.int32)
    depths = jnp.sum(jnp.where(ordinal[None, :] <= ordinal[:, None], deeper[None, :], 0), 1)
    first = row * ROW
    shard = first + chip * CORES + core
    asked = jnp.stack([shard, shard + 1 - 2 * core, first, first + ROW])
    own_depth = jnp.sum(
        jnp.where(ordinal[None, :] <= asked[:, None], deeper[None, :], 0), 1
    ) + (asked >= count)
    wanted = own_depth[:, None] - 1 - levels[None, :]
    match = (depths[None, None, :] == wanted[:, :, None]) & (
        ordinal[None, None, :] < asked[:, None, None]
    )
    elder = jnp.max(jnp.where(match, ordinal[None, None, :], -1), 2)
    mine, stack, relay = elder[:2], elder[2], elder[3]
    in_row = 2 * (chip - (mine - first) // CORES) + mine % CORES
    holder = CHIPS - 1 - jnp.sum(
        jnp.where(mine[:, :, None] == stack[None, None, :], levels, 0), 2
    )
    code = jnp.where(mine >= first, in_row, 2 * CHIPS + holder - chip)
    code = jnp.clip(jnp.where(mine >= 0, code, 0), 0, 3 * CHIPS - 1)
    code = jnp.concatenate([jnp.stack([core, 1 - core])[:, None], code], 1).reshape(-1)
    held = jnp.sum(jnp.where(levels == CHIPS - 1 - chip, relay, 0))
    far = (held - first) // CORES - chip
    send = jnp.clip(2 * far + held % CORES, 0, 2 * CHIPS - 3)
    held = jnp.stack([CHIPS - 1 - chip, CHIPS - chip, jnp.where(chip == 2, CHIPS - 1, CHIPS)])
    node = jnp.sum(jnp.where(held[:, None] == levels[None, :], relay[None, :], 0), 1)
    here = (held < LEVELS) & (node >= first) & ((node - first) // CORES == chip)
    land = jnp.where(here, node % CORES, CORES)
    table = jnp.concatenate(
        [code, (elder[0] >= 0).astype(jnp.int32), send[None], land, core[None]]
    ).astype(jnp.int32)
    slot_depth = own_depth[0] - jnp.arange(SLOTS, dtype=jnp.int32)
    pair_depth = jnp.where(core == 0, own_depth[:2], own_depth[1::-1])
    return table, slot_depth, pair_depth


def angles_of(depth):
    frequency = jnp.exp(jnp.arange(HALF, dtype=F32) * (-2.0 * math.log(BASE) / HD))
    position = (depth[:, None] * TOK + jnp.arange(TOK, dtype=jnp.int32)[None, :]).reshape(-1)
    return position.astype(F32)[:, None] * frequency[None, :]


def turn(block, cosine, sine):
    first, second = block[:, :HALF], block[:, HALF:]
    return jnp.concatenate(
        [first * cosine - second * sine, second * cosine + first * sine], -1
    )


def fetch(code, sources, target, sem):
    at = 0
    for ref in sources:
        for half in range(ref.shape[0] // TOK):

            @pl.when(code == at)
            def _(ref=ref, half=half):
                pltpu.make_async_copy(ref.at[pl.ds(half * TOK, TOK)], target, sem).start()

            at += 1


def await_fetch(sources, target, sem):
    pltpu.make_async_copy(sources[0].at[pl.ds(0, TOK)], target, sem).wait()


def part(ref, i):
    return ref.at[pl.ds(i * TOK, TOK)]


def pick_kernel(offset, number, table, *refs):
    sources, (o_ref, sem) = refs[:-2], refs[-2:]
    for i in range(number):
        fetch(table[offset + i], sources, part(o_ref, i), sem.at[i])
    for i in range(number):
        await_fetch(sources, part(o_ref, i), sem.at[i])


def call_pick(table, sources, offset, number):
    return pl.pallas_call(
        functools.partial(pick_kernel, offset, number),
        compiler_params=room(4),
        out_shape=jax.ShapeDtypeStruct((number * TOK, HD), BF16),
        in_specs=[SMEM] + [ANY] * len(sources),
        out_specs=VMEM,
        scratch_shapes=[pltpu.SemaphoreType.DMA((number,))],
    )(table, *sources)


NT = (((1,), (1,)), ((), ()))
NN = (((1,), (0,)), ((), ()))
TN = (((0,), (0,)), ((), ()))


def dot(a, b, dims):
    return lax.dot_general(a, b, dims, preferred_element_type=F32)


def attend_kernel(table, qg_hbm, cos_hbm, sin_hbm, other_hbm, *refs):
    sources = refs[: 2 * CHIPS]
    out_hbm, keep_hbm, give_hbm = refs[2 * CHIPS : 2 * CHIPS + 3]
    (qg_ref, cos_ref, sin_ref, mine_ref, other_ref, keys, vals, q_all, low_all, score_all) = refs[
        2 * CHIPS + 3 : 2 * CHIPS + 13
    ]
    out_ref, keep_ref, give_ref, sem, in_sem, out_sem = refs[2 * CHIPS + 13 :]
    whole_in = [
        pltpu.make_async_copy(src, dst, in_sem.at[i])
        for i, (src, dst) in enumerate(
            ((qg_hbm, qg_ref), (cos_hbm, cos_ref), (sin_hbm, sin_ref))
        )
    ]
    other_in = [
        pltpu.make_async_copy(part(other_hbm, i), part(other_ref, i), sem.at[SLOTS + i])
        for i in range(SLOTS)
    ]
    for copy in whole_in:
        copy.start()
    for i in range(SLOTS):
        fetch(table[OWN + i], sources, part(mine_ref, i), sem.at[i])
        other_in[i].start()
    for copy in whole_in:
        copy.wait()
    for h in range(2):
        q_all[h * TOK : (h + 1) * TOK, :] = turn(
            qg_ref[:, h * HD : (h + 1) * HD].astype(F32), cos_ref[:TOK, :], sin_ref[:TOK, :]
        ).astype(BF16)
    is_key = table[CORE] == 0
    for i in range(SLOTS):
        here = slice(i * TOK, (i + 1) * TOK)
        await_fetch(sources, part(mine_ref, i), sem.at[i])
        other_in[i].wait()
        mine, other = mine_ref[here, :], other_ref[here, :]
        keys[here, :] = turn(
            jnp.where(is_key, mine, other).astype(F32), cos_ref[here, :], sin_ref[here, :]
        ).astype(BF16)
        vals[here, :] = jnp.where(is_key, other, mine)
    scaling = HD**-0.5
    earlier = lax.broadcasted_iota(jnp.int32, (TOK, TOK), 1) <= lax.broadcasted_iota(
        jnp.int32, (TOK, TOK), 0
    )
    last = SLOTS - 1
    block = lambda ref, i: ref[i * TOK : (i + 1) * TOK, :]
    for h in range(2):
        rows = slice(h * TOK, (h + 1) * TOK)
        q, g = q_all[rows, :], qg_ref[:, WIDE + h * HD : WIDE + (h + 1) * HD]

        def joint(a, which, fill):
            parts = [dot(a, block(which, i), NT) for i in range(SLOTS)]
            if fill is None:
                return [jnp.where(earlier, parts[0], parts[last])] + parts[1:last]
            parts = [parts[0] * scaling] + [
                jnp.where(table[SEEN + i - 1] > 0, parts[i] * scaling, fill)
                for i in range(1, SLOTS)
            ]
            return [jnp.where(earlier, parts[0], parts[last])] + parts[1:last]

        scores = joint(q, keys, -1e30)
        top = functools.reduce(jnp.maximum, scores)
        top = jnp.max(top, -1, keepdims=True)
        raw = [jnp.exp(s - top) for s in scores]
        share = 1.0 / jnp.sum(functools.reduce(jnp.add, raw), -1, keepdims=True)
        probs = [r * share for r in raw]
        grads = joint(g, vals, None)
        delta = functools.reduce(jnp.add, [p * d for p, d in zip(probs, grads)])
        delta = jnp.sum(delta, -1, keepdims=True)
        for ref, parts in (
            (low_all, probs),
            (score_all, [p * (d - delta) * scaling for p, d in zip(probs, grads)]),
        ):
            ref[rows, :TOK] = jnp.where(earlier, parts[0], 0.0).astype(BF16)
            ref[rows, last * TOK :] = jnp.where(earlier, 0.0, parts[0]).astype(BF16)
            for i in range(1, last):
                ref[rows, i * TOK : (i + 1) * TOK] = parts[i].astype(BF16)
        out_ref[:, h * HD : (h + 1) * HD] = dot(low_all[rows, :], vals[...], NN).astype(BF16)
        out_ref[:, WIDE + h * HD : WIDE + (h + 1) * HD] = turn(
            dot(score_all[rows, :], keys[...], NN), cos_ref[:TOK, :], -sin_ref[:TOK, :]
        ).astype(BF16)
    outgoing = [pltpu.make_async_copy(out_ref, out_hbm, out_sem.at[0])]
    outgoing[0].start()
    for i in range(SLOTS):
        cols = slice(i * TOK, (i + 1) * TOK)
        part_key = dot(score_all[:, cols], q_all[...], TN)
        part_value = dot(low_all[:TOK, cols], qg_ref[:, WIDE : WIDE + HD], TN) + dot(
            low_all[TOK:, cols], qg_ref[:, WIDE + HD :], TN
        )
        keep_ref[cols, :] = jnp.where(is_key, part_key, part_value).astype(BF16)
        give_ref[cols, :] = jnp.where(is_key, part_value, part_key).astype(BF16)
        for k, (src, dst) in enumerate(((give_ref, give_hbm), (keep_ref, keep_hbm))):
            outgoing.append(
                pltpu.make_async_copy(part(src, i), part(dst, i), out_sem.at[1 + 2 * i + k])
            )
            outgoing[-1].start()
    for copy in outgoing:
        copy.wait()


def call_attend(table, query_grad, cosine, sine, other, sources):
    return pl.pallas_call(
        attend_kernel,
        out_shape=(
            jax.ShapeDtypeStruct((TOK, 2 * WIDE), BF16),
            jax.ShapeDtypeStruct((KEYS, HD), BF16),
            jax.ShapeDtypeStruct((KEYS, HD), BF16),
        ),
        in_specs=[SMEM] + [ANY] * (4 + len(sources)),
        out_specs=(ANY,) * 3,
        scratch_shapes=[
            pltpu.VMEM((TOK, 2 * WIDE), BF16),
            pltpu.VMEM((KEYS, HALF), F32),
            pltpu.VMEM((KEYS, HALF), F32),
            pltpu.VMEM((KEYS, HD), BF16),
            pltpu.VMEM((KEYS, HD), BF16),
            pltpu.VMEM((KEYS, HD), BF16),
            pltpu.VMEM((KEYS, HD), BF16),
            pltpu.VMEM((2 * TOK, HD), BF16),
            pltpu.VMEM((2 * TOK, KEYS), BF16),
            pltpu.VMEM((2 * TOK, KEYS), BF16),
            pltpu.VMEM((TOK, 2 * WIDE), BF16),
            pltpu.VMEM((KEYS, HD), BF16),
            pltpu.VMEM((KEYS, HD), BF16),
            pltpu.SemaphoreType.DMA((2 * SLOTS,)),
            pltpu.SemaphoreType.DMA((3,)),
            pltpu.SemaphoreType.DMA((1 + 2 * SLOTS,)),
        ],
    )(table, query_grad, cosine, sine, other, *sources)


def spread_kernel(table, keep_hbm, got_hbm, *refs):
    outs, (total, terms, sem) = refs[:-3], refs[-3:]
    copies = [
        [
            pltpu.make_async_copy(part(src, i), part(terms.at[k], i), sem.at[k, i])
            for i in range(SLOTS)
        ]
        for k, src in enumerate((keep_hbm, got_hbm))
    ]
    for group in copies:
        for copy in group:
            copy.start()
    total[...] = jnp.zeros_like(total)
    for k, offset in enumerate((OWN, OTHER)):
        source = terms.at[k]
        for i in range(SLOTS):
            copies[k][i].wait()
            at = pl.ds(pl.multiple_of(table[offset + i] * TOK, TOK), TOK)
            total[at, :] += source[i * TOK : (i + 1) * TOK, :].astype(F32)
    for k in range(CHIPS):
        outs[k][...] = total[k * PAIR : (k + 1) * PAIR, :].astype(outs[k].dtype)
        low = CHIPS * PAIR + k * TOK
        outs[CHIPS + k][...] = total[low : low + TOK, :].astype(BF16)


def call_spread(table, keep, got):
    return pl.pallas_call(
        spread_kernel,
        compiler_params=room(12),
        out_shape=tuple(
            [jax.ShapeDtypeStruct((PAIR, HD), F32)]
            + [jax.ShapeDtypeStruct((PAIR, HD), BF16)] * (CHIPS - 1)
            + [jax.ShapeDtypeStruct((TOK, HD), BF16)] * CHIPS
        ),
        in_specs=[SMEM, ANY, ANY],
        out_specs=(VMEM,) * (2 * CHIPS),
        scratch_shapes=[
            pltpu.VMEM((CHIPS * PAIR + CHIPS * TOK, HD), F32),
            pltpu.VMEM((CORES, KEYS, HD), BF16),
            pltpu.SemaphoreType.DMA((CORES, SLOTS)),
        ],
    )(table, keep, got)


def sum_kernel(*refs):
    total = refs[0][...].astype(F32)
    for ref in refs[1:-1]:
        total = total + ref[...].astype(F32)
    refs[-1][...] = total.astype(refs[-1].dtype)


def call_sum(parts, dtype):
    return pl.pallas_call(
        sum_kernel,
        compiler_params=room(6),
        out_shape=jax.ShapeDtypeStruct(parts[0].shape, dtype),
        in_specs=[VMEM] * len(parts),
        out_specs=VMEM,
    )(*parts)


def close_kernel(table, own_ref, *refs):
    backs = refs[:-4]
    cos_ref, sin_ref, o_ref, total = refs[-4:]
    total[...] = own_ref[...]
    for k, back in enumerate(backs):
        code = table[LAND + k]

        @pl.when(code < CORES)
        def _(back=back, code=code):
            at = pl.ds(pl.multiple_of(code * TOK, TOK), TOK)
            total[at, :] += back[...].astype(F32)

    is_key = table[CORE] == 0

    @pl.when(is_key)
    def _():
        o_ref[...] = turn(total[...], cos_ref[...], -sin_ref[...]).astype(BF16)

    @pl.when(jnp.logical_not(is_key))
    def _():
        o_ref[...] = total[...].astype(BF16)


def call_close(table, own, backs, cosine, sine):
    return pl.pallas_call(
        close_kernel,
        compiler_params=room(8),
        out_shape=jax.ShapeDtypeStruct((PAIR, HD), BF16),
        in_specs=[SMEM] + [VMEM] * (3 + len(backs)),
        out_specs=VMEM,
        scratch_shapes=[pltpu.VMEM((PAIR, HD), F32)],
    )(table, own, *backs, cosine, sine)


def along(block, shift, starts=range(CHIPS)):
    return lax.ppermute(
        block, "chip", [(i, i + shift) for i in starts if 0 <= i + shift < CHIPS]
    )


def next_row(block, shift):
    rows = lax.axis_size("row")
    return lax.ppermute(
        block, "row", [(i, i + shift) for i in range(rows) if 0 <= i + shift < rows]
    )


def swap(block):
    return lax.ppermute(block, "core", [(0, 1), (1, 0)])


def shards(queries, keys, values, grad_attn, parent_gap):
    row, chip, core = (lax.axis_index(name) for name in ("row", "chip", "core"))
    tokens = queries.shape[0]
    both = lax.all_to_all(
        jnp.concatenate([keys, values], 1),
        ("core", "head"),
        split_axis=1,
        concat_axis=0,
        tiled=True,
    )
    table, slot_depth, pair_depth = plan(parent_gap, row, chip, core)
    pair_angles = angles_of(pair_depth)
    pair_cos, pair_sin = jnp.cos(pair_angles), jnp.sin(pair_angles)
    table, pair_cos, pair_sin = lax.optimization_barrier((table, pair_cos, pair_sin))
    pairs = [both, along(both, -1), along(both, -2, (2,))]
    held, slot_depth = lax.optimization_barrier(
        (call_pick(table, pairs, SEND, 1), slot_depth)
    )
    relay = next_row(held, 1)
    slot_angles = angles_of(slot_depth)
    slot_cos, slot_sin = jnp.cos(slot_angles), jnp.sin(slot_angles)
    relay, slot_cos, slot_sin = lax.optimization_barrier((relay, slot_cos, slot_sin))
    sources = [both] + [along(both, k) for k in (1, 2, 3)]
    query_grad = jnp.concatenate(
        [queries.reshape(tokens, HEADS, WIDE), grad_attn.reshape(tokens, HEADS, WIDE)], 2
    ).reshape(tokens, HEADS * 2 * WIDE)
    query_grad = lax.all_to_all(query_grad, "head", split_axis=1, concat_axis=0, tiled=True)
    sources += [relay] + [along(relay, -k) for k in (1, 2, 3)]
    other = swap(call_pick(table, sources, OTHER, SLOTS))
    out, keep, give = call_attend(table, query_grad, slot_cos, slot_sin, other, sources)
    got = swap(give)
    out = lax.all_to_all(out, "head", split_axis=0, concat_axis=1, tiled=True)
    spread = call_spread(table, keep, got)
    own, within, stack = spread[0], spread[1:CHIPS], spread[CHIPS:]
    stack_sum = call_sum([stack[0]] + [along(stack[k], k) for k in (1, 2, 3)], BF16)
    back = next_row(stack_sum, -1)
    own = call_sum([own] + [along(within[k - 1], -k) for k in (1, 2, 3)], F32)
    backs = [back, along(back, 1), along(back, 2, (0,))]
    grad_both = call_close(table, own, backs, pair_cos, pair_sin)
    grad_both, out = lax.optimization_barrier((grad_both, out))
    grad_both = lax.all_to_all(grad_both, ("core", "head"), split_axis=0, concat_axis=1, tiled=True)
    out = out.reshape(tokens, HEADS, 2, WIDE)
    attended = out[:, :, 0].reshape(tokens, HEADS * WIDE)
    grad_query = out[:, :, 1].reshape(tokens, HEADS * WIDE)
    half = HEADS * HD
    return attended, grad_query, grad_both[:, :half], grad_both[:, half:]


def solution(mesh):
    devices = mesh.devices
    rows = devices.shape[0] // ROW
    split = Mesh(
        devices.reshape(rows, CHIPS, CORES, devices.shape[1]), ("row", "chip", "core", "head")
    )
    spec = P(("row", "chip", "core", "head"), None)

    return jax.shard_map(
        shards,
        mesh=split,
        in_specs=(spec, spec, spec, spec, P()),
        out_specs=(spec, spec, spec, spec),
        check_vma=False,
    )
```

```python
import functools
import math

import jax
import jax.numpy as jnp
from jax import lax
from jax.experimental import pallas as pl
from jax.experimental.pallas import tpu as pltpu
from jax.sharding import Mesh
from jax.sharding import PartitionSpec as P


HD = 256
HALF = HD // 2
TOK = 256
LEVELS = 4
SLOTS = LEVELS + 1
CHIPS = 4
CORES = 2
PAIR = CORES * TOK
KEYS = SLOTS * TOK
ROW = CHIPS * CORES
HEADS = 4
WIDE = 2 * HD
OWN, OTHER, SEEN, SEND, LAND, CORE, DEPTHS, PAIRS, TABLE = 0, 5, 10, 14, 15, 18, 19, 24, 32
BASE = 10000.0
BF16 = jnp.bfloat16
F32 = jnp.float32

MIB = 1024 * 1024


def room(mib):
    return pltpu.CompilerParams(vmem_limit_bytes=mib * MIB)


ANY = pl.BlockSpec(memory_space=pl.ANY)
VMEM = pl.BlockSpec(memory_space=pltpu.VMEM)
SMEM = pl.BlockSpec(memory_space=pltpu.SMEM)


def plan_kernel(gap_ref, table):
    row, chip, core = (lax.axis_index(name) for name in ("row", "chip", "core"))
    count = gap_ref.shape[0]
    first = row * ROW
    shard = first + chip * CORES + core
    pick = lambda cond, a, b: jnp.where(cond, a, b)

    def gap_of(node):
        inside = gap_ref[jnp.clip(node, 0, count - 1)]
        return pick(node >= count, 1, pick(node < 0, 0, inside))

    def elders_of(node):
        found = []
        for _ in range(LEVELS):
            gap = gap_of(node)
            node = pick(gap > 0, node - gap, -1)
            found.append(node)
        return found

    def deeper(node, depth):
        return depth + pick(gap_ref[node] == 1, 1, 0)

    depth = lax.fori_loop(0, first + chip * CORES + 1, deeper, jnp.int32(0))
    pair_depth = [depth, deeper(first + chip * CORES + 1, depth)]
    own_depth = pick(core == 0, pair_depth[0], pair_depth[1])
    stack, relay = elders_of(first), elders_of(first + ROW)
    for start, node, half in (
        (OWN, shard, core),
        (OTHER, shard + 1 - 2 * core, 1 - core),
    ):
        table[start] = half
        for i, elder in enumerate(elders_of(node)):
            in_row = 2 * (chip - ((elder - first) >> 1)) + (elder & 1)
            before = jnp.int32(0)
            for j in range(LEVELS):
                before = pick(elder == stack[j], 3 * CHIPS - 1 - j - chip, before)
            code = pick(elder < 0, 0, pick(elder >= first, in_row, before))
            table[start + 1 + i] = jnp.clip(code, 0, 3 * CHIPS - 1)
            if start == OWN:
                table[SEEN + i] = pick(elder >= 0, 1, 0)

    def held(rank):
        node = jnp.int32(-1)
        for j in range(LEVELS):
            node = pick(rank == j, relay[j], node)
        return node

    node = held(CHIPS - 1 - chip)
    code = 2 * (((node - first) >> 1) - chip) + (node & 1)
    table[SEND] = jnp.clip(code, 0, 2 * CHIPS - 3)
    for i, rank in enumerate((CHIPS - 1 - chip, CHIPS - chip, pick(chip == 2, CHIPS - 1, CHIPS))):
        node = held(rank)
        here = (node >= first) & (((node - first) >> 1) == chip)
        table[LAND + i] = pick(here, node & 1, CORES)
    table[CORE] = core
    for i in range(SLOTS):
        table[DEPTHS + i] = own_depth - i
    for i in range(CORES):
        table[PAIRS + i] = pair_depth[i]
    for i in range(PAIRS + CORES, TABLE):
        table[i] = 0


def call_plan(parent_gap):
    return pl.pallas_call(
        plan_kernel,
        out_shape=jax.ShapeDtypeStruct((TABLE,), jnp.int32),
        in_specs=[SMEM],
        out_specs=SMEM,
    )(parent_gap)


def angles_of(depth):
    frequency = jnp.exp(jnp.arange(HALF, dtype=F32) * (-2.0 * math.log(BASE) / HD))
    position = (depth[:, None] * TOK + jnp.arange(TOK, dtype=jnp.int32)[None, :]).reshape(-1)
    return position.astype(F32)[:, None] * frequency[None, :]


def turn(block, cosine, sine):
    first, second = block[:, :HALF], block[:, HALF:]
    return jnp.concatenate(
        [first * cosine - second * sine, second * cosine + first * sine], -1
    )


def fetch(code, sources, target, sem):
    at = 0
    for ref in sources:
        for half in range(ref.shape[0] // TOK):

            @pl.when(code == at)
            def _(ref=ref, half=half):
                pltpu.make_async_copy(ref.at[pl.ds(half * TOK, TOK)], target, sem).start()

            at += 1


def await_fetch(sources, target, sem):
    pltpu.make_async_copy(sources[0].at[pl.ds(0, TOK)], target, sem).wait()


def part(ref, i):
    return ref.at[pl.ds(i * TOK, TOK)]


def pick_kernel(offset, number, table, *refs):
    sources, (o_ref, sem) = refs[:-2], refs[-2:]
    for i in range(number):
        fetch(table[offset + i], sources, part(o_ref, i), sem.at[i])
    for i in range(number):
        await_fetch(sources, part(o_ref, i), sem.at[i])


def call_pick(table, sources, offset, number):
    return pl.pallas_call(
        functools.partial(pick_kernel, offset, number),
        compiler_params=room(4),
        out_shape=jax.ShapeDtypeStruct((number * TOK, HD), BF16),
        in_specs=[SMEM] + [ANY] * len(sources),
        out_specs=VMEM,
        scratch_shapes=[pltpu.SemaphoreType.DMA((number,))],
    )(table, *sources)


NT = (((1,), (1,)), ((), ()))
NN = (((1,), (0,)), ((), ()))
TN = (((0,), (0,)), ((), ()))


def dot(a, b, dims):
    return lax.dot_general(a, b, dims, preferred_element_type=F32)


def attend_kernel(table, qg_hbm, cos_hbm, sin_hbm, other_hbm, *refs):
    sources = refs[: 2 * CHIPS]
    out_hbm, keep_hbm, give_hbm = refs[2 * CHIPS : 2 * CHIPS + 3]
    (qg_ref, cos_ref, sin_ref, mine_ref, other_ref, keys, vals, q_all, low_all, score_all) = refs[
        2 * CHIPS + 3 : 2 * CHIPS + 13
    ]
    out_ref, keep_ref, give_ref, sem, in_sem, out_sem = refs[2 * CHIPS + 13 :]
    whole_in = [
        pltpu.make_async_copy(src, dst, in_sem.at[i])
        for i, (src, dst) in enumerate(
            ((qg_hbm, qg_ref), (cos_hbm, cos_ref), (sin_hbm, sin_ref))
        )
    ]
    other_in = [
        pltpu.make_async_copy(part(other_hbm, i), part(other_ref, i), sem.at[SLOTS + i])
        for i in range(SLOTS)
    ]
    for copy in whole_in:
        copy.start()
    for i in range(SLOTS):
        fetch(table[OWN + i], sources, part(mine_ref, i), sem.at[i])
        other_in[i].start()
    for copy in whole_in:
        copy.wait()
    for h in range(2):
        q_all[h * TOK : (h + 1) * TOK, :] = turn(
            qg_ref[:, h * HD : (h + 1) * HD].astype(F32), cos_ref[:TOK, :], sin_ref[:TOK, :]
        ).astype(BF16)
    is_key = table[CORE] == 0
    for i in range(SLOTS):
        here = slice(i * TOK, (i + 1) * TOK)
        await_fetch(sources, part(mine_ref, i), sem.at[i])
        other_in[i].wait()
        mine, other = mine_ref[here, :], other_ref[here, :]
        keys[here, :] = turn(
            jnp.where(is_key, mine, other).astype(F32), cos_ref[here, :], sin_ref[here, :]
        ).astype(BF16)
        vals[here, :] = jnp.where(is_key, other, mine)
    scaling = HD**-0.5
    earlier = lax.broadcasted_iota(jnp.int32, (TOK, TOK), 1) <= lax.broadcasted_iota(
        jnp.int32, (TOK, TOK), 0
    )
    last = SLOTS - 1
    block = lambda ref, i: ref[i * TOK : (i + 1) * TOK, :]
    for h in range(2):
        rows = slice(h * TOK, (h + 1) * TOK)
        q, g = q_all[rows, :], qg_ref[:, WIDE + h * HD : WIDE + (h + 1) * HD]

        def joint(a, which, fill):
            parts = [dot(a, block(which, i), NT) for i in range(SLOTS)]
            if fill is None:
                return [jnp.where(earlier, parts[0], parts[last])] + parts[1:last]
            parts = [parts[0] * scaling] + [
                jnp.where(table[SEEN + i - 1] > 0, parts[i] * scaling, fill)
                for i in range(1, SLOTS)
            ]
            return [jnp.where(earlier, parts[0], parts[last])] + parts[1:last]

        scores = joint(q, keys, -1e30)
        top = functools.reduce(jnp.maximum, scores)
        top = jnp.max(top, -1, keepdims=True)
        raw = [jnp.exp(s - top) for s in scores]
        share = 1.0 / jnp.sum(functools.reduce(jnp.add, raw), -1, keepdims=True)
        probs = [r * share for r in raw]
        grads = joint(g, vals, None)
        delta = functools.reduce(jnp.add, [p * d for p, d in zip(probs, grads)])
        delta = jnp.sum(delta, -1, keepdims=True)
        for ref, parts in (
            (low_all, probs),
            (score_all, [p * (d - delta) * scaling for p, d in zip(probs, grads)]),
        ):
            ref[rows, :TOK] = jnp.where(earlier, parts[0], 0.0).astype(BF16)
            ref[rows, last * TOK :] = jnp.where(earlier, 0.0, parts[0]).astype(BF16)
            for i in range(1, last):
                ref[rows, i * TOK : (i + 1) * TOK] = parts[i].astype(BF16)
        out_ref[:, h * HD : (h + 1) * HD] = dot(low_all[rows, :], vals[...], NN).astype(BF16)
        out_ref[:, WIDE + h * HD : WIDE + (h + 1) * HD] = turn(
            dot(score_all[rows, :], keys[...], NN), cos_ref[:TOK, :], -sin_ref[:TOK, :]
        ).astype(BF16)
    outgoing = [pltpu.make_async_copy(out_ref, out_hbm, out_sem.at[0])]
    outgoing[0].start()
    for i in range(SLOTS):
        cols = slice(i * TOK, (i + 1) * TOK)
        part_key = dot(score_all[:, cols], q_all[...], TN)
        part_value = dot(low_all[:TOK, cols], qg_ref[:, WIDE : WIDE + HD], TN) + dot(
            low_all[TOK:, cols], qg_ref[:, WIDE + HD :], TN
        )
        keep_ref[cols, :] = jnp.where(is_key, part_key, part_value).astype(BF16)
        give_ref[cols, :] = jnp.where(is_key, part_value, part_key).astype(BF16)
        for k, (src, dst) in enumerate(((give_ref, give_hbm), (keep_ref, keep_hbm))):
            outgoing.append(
                pltpu.make_async_copy(part(src, i), part(dst, i), out_sem.at[1 + 2 * i + k])
            )
            outgoing[-1].start()
    for copy in outgoing:
        copy.wait()


def call_attend(table, query_grad, cosine, sine, other, sources):
    return pl.pallas_call(
        attend_kernel,
        compiler_params=room(24),
        out_shape=(
            jax.ShapeDtypeStruct((TOK, 2 * WIDE), BF16),
            jax.ShapeDtypeStruct((KEYS, HD), BF16),
            jax.ShapeDtypeStruct((KEYS, HD), BF16),
        ),
        in_specs=[SMEM] + [ANY] * (4 + len(sources)),
        out_specs=(ANY,) * 3,
        scratch_shapes=[
            pltpu.VMEM((TOK, 2 * WIDE), BF16),
            pltpu.VMEM((KEYS, HALF), F32),
            pltpu.VMEM((KEYS, HALF), F32),
            pltpu.VMEM((KEYS, HD), BF16),
            pltpu.VMEM((KEYS, HD), BF16),
            pltpu.VMEM((KEYS, HD), BF16),
            pltpu.VMEM((KEYS, HD), BF16),
            pltpu.VMEM((2 * TOK, HD), BF16),
            pltpu.VMEM((2 * TOK, KEYS), BF16),
            pltpu.VMEM((2 * TOK, KEYS), BF16),
            pltpu.VMEM((TOK, 2 * WIDE), BF16),
            pltpu.VMEM((KEYS, HD), BF16),
            pltpu.VMEM((KEYS, HD), BF16),
            pltpu.SemaphoreType.DMA((2 * SLOTS,)),
            pltpu.SemaphoreType.DMA((3,)),
            pltpu.SemaphoreType.DMA((1 + 2 * SLOTS,)),
        ],
    )(table, query_grad, cosine, sine, other, *sources)


def spread_kernel(table, keep_hbm, got_hbm, *refs):
    outs, (total, terms, sem) = refs[:-3], refs[-3:]
    copies = [
        [
            pltpu.make_async_copy(part(src, i), part(terms.at[k], i), sem.at[k, i])
            for i in range(SLOTS)
        ]
        for k, src in enumerate((keep_hbm, got_hbm))
    ]
    for group in copies:
        for copy in group:
            copy.start()
    total[...] = jnp.zeros_like(total)
    for k, offset in enumerate((OWN, OTHER)):
        source = terms.at[k]
        for i in range(SLOTS):
            copies[k][i].wait()
            at = pl.ds(pl.multiple_of(table[offset + i] * TOK, TOK), TOK)
            total[at, :] += source[i * TOK : (i + 1) * TOK, :].astype(F32)
    for k in range(CHIPS):
        outs[k][...] = total[k * PAIR : (k + 1) * PAIR, :].astype(outs[k].dtype)
        low = CHIPS * PAIR + k * TOK
        outs[CHIPS + k][...] = total[low : low + TOK, :].astype(BF16)


def call_spread(table, keep, got):
    return pl.pallas_call(
        spread_kernel,
        compiler_params=room(12),
        out_shape=tuple(
            [jax.ShapeDtypeStruct((PAIR, HD), F32)]
            + [jax.ShapeDtypeStruct((PAIR, HD), BF16)] * (CHIPS - 1)
            + [jax.ShapeDtypeStruct((TOK, HD), BF16)] * CHIPS
        ),
        in_specs=[SMEM, ANY, ANY],
        out_specs=(VMEM,) * (2 * CHIPS),
        scratch_shapes=[
            pltpu.VMEM((CHIPS * PAIR + CHIPS * TOK, HD), F32),
            pltpu.VMEM((CORES, KEYS, HD), BF16),
            pltpu.SemaphoreType.DMA((CORES, SLOTS)),
        ],
    )(table, keep, got)


def sum_kernel(*refs):
    total = refs[0][...].astype(F32)
    for ref in refs[1:-1]:
        total = total + ref[...].astype(F32)
    refs[-1][...] = total.astype(refs[-1].dtype)


def call_sum(parts, dtype):
    return pl.pallas_call(
        sum_kernel,
        compiler_params=room(6),
        out_shape=jax.ShapeDtypeStruct(parts[0].shape, dtype),
        in_specs=[VMEM] * len(parts),
        out_specs=VMEM,
    )(*parts)


def close_kernel(table, own_ref, *refs):
    backs = refs[:-4]
    cos_ref, sin_ref, o_ref, total = refs[-4:]
    total[...] = own_ref[...]
    for k, back in enumerate(backs):
        code = table[LAND + k]

        @pl.when(code < CORES)
        def _(back=back, code=code):
            at = pl.ds(pl.multiple_of(code * TOK, TOK), TOK)
            total[at, :] += back[...].astype(F32)

    is_key = table[CORE] == 0

    @pl.when(is_key)
    def _():
        o_ref[...] = turn(total[...], cos_ref[...], -sin_ref[...]).astype(BF16)

    @pl.when(jnp.logical_not(is_key))
    def _():
        o_ref[...] = total[...].astype(BF16)


def call_close(table, own, backs, cosine, sine):
    return pl.pallas_call(
        close_kernel,
        compiler_params=room(8),
        out_shape=jax.ShapeDtypeStruct((PAIR, HD), BF16),
        in_specs=[SMEM] + [VMEM] * (3 + len(backs)),
        out_specs=VMEM,
        scratch_shapes=[pltpu.VMEM((PAIR, HD), F32)],
    )(table, own, *backs, cosine, sine)


def along(block, shift, starts=range(CHIPS)):
    return lax.ppermute(
        block, "chip", [(i, i + shift) for i in starts if 0 <= i + shift < CHIPS]
    )


def next_row(block, shift):
    rows = lax.axis_size("row")
    return lax.ppermute(
        block, "row", [(i, i + shift) for i in range(rows) if 0 <= i + shift < rows]
    )


def swap(block):
    return lax.ppermute(block, "core", [(0, 1), (1, 0)])


def shards(queries, keys, values, grad_attn, parent_gap):
    tokens = queries.shape[0]
    both = lax.all_to_all(
        jnp.concatenate([keys, values], 1),
        ("core", "head"),
        split_axis=1,
        concat_axis=0,
        tiled=True,
    )
    table = call_plan(parent_gap)
    slot_depth, pair_depth = table[DEPTHS : DEPTHS + SLOTS], table[PAIRS : PAIRS + CORES]
    pair_angles = angles_of(pair_depth)
    pair_cos, pair_sin = jnp.cos(pair_angles), jnp.sin(pair_angles)
    table, pair_cos, pair_sin = lax.optimization_barrier((table, pair_cos, pair_sin))
    pairs = [both, along(both, -1), along(both, -2, (2,))]
    query_grad = jnp.concatenate(
        [queries.reshape(tokens, HEADS, WIDE), grad_attn.reshape(tokens, HEADS, WIDE)], 2
    ).reshape(tokens, HEADS * 2 * WIDE)
    query_grad = lax.all_to_all(query_grad, "head", split_axis=1, concat_axis=0, tiled=True)
    held, slot_depth = lax.optimization_barrier(
        (call_pick(table, pairs, SEND, 1), slot_depth)
    )
    relay = next_row(held, 1)
    slot_angles = angles_of(slot_depth)
    slot_cos, slot_sin = jnp.cos(slot_angles), jnp.sin(slot_angles)
    relay, slot_cos, slot_sin, query_grad = lax.optimization_barrier(
        (relay, slot_cos, slot_sin, query_grad)
    )
    sources = [both] + [along(both, k) for k in (1, 2, 3)]
    sources += [relay] + [along(relay, -k) for k in (1, 2, 3)]
    other = swap(call_pick(table, sources, OTHER, SLOTS))
    out, keep, give = call_attend(table, query_grad, slot_cos, slot_sin, other, sources)
    got = swap(give)
    out = lax.all_to_all(out, "head", split_axis=0, concat_axis=1, tiled=True)
    spread = call_spread(table, keep, got)
    own, within, stack = spread[0], spread[1:CHIPS], spread[CHIPS:]
    stack_sum = call_sum([stack[0]] + [along(stack[k], k) for k in (1, 2, 3)], BF16)
    back = next_row(stack_sum, -1)
    own = call_sum([own] + [along(within[k - 1], -k) for k in (1, 2, 3)], F32)
    backs = [back, along(back, 1), along(back, 2, (0,))]
    grad_both = call_close(table, own, backs, pair_cos, pair_sin)
    grad_both, out = lax.optimization_barrier((grad_both, out))
    grad_both = lax.all_to_all(grad_both, ("core", "head"), split_axis=0, concat_axis=1, tiled=True)
    out = out.reshape(tokens, HEADS, 2, WIDE)
    attended = out[:, :, 0].reshape(tokens, HEADS * WIDE)
    grad_query = out[:, :, 1].reshape(tokens, HEADS * WIDE)
    half = HEADS * HD
    return attended, grad_query, grad_both[:, :half], grad_both[:, half:]


def solution(mesh):
    devices = mesh.devices
    rows = devices.shape[0] // ROW
    split = Mesh(
        devices.reshape(rows, CHIPS, CORES, devices.shape[1]), ("row", "chip", "core", "head")
    )
    spec = P(("row", "chip", "core", "head"), None)

    return jax.shard_map(
        shards,
        mesh=split,
        in_specs=(spec, spec, spec, spec, P()),
        out_specs=(spec, spec, spec, spec),
        check_vma=False,
    )
```

```python
import functools
import math

import jax
import jax.numpy as jnp
from jax import lax
from jax.experimental import pallas as pl
from jax.experimental.pallas import tpu as pltpu
from jax.sharding import Mesh
from jax.sharding import PartitionSpec as P


HD = 256
HALF = HD // 2
TOK = 256
LEVELS = 4
SLOTS = LEVELS + 1
CHIPS = 4
CORES = 2
PAIR = CORES * TOK
KEYS = SLOTS * TOK
ROW = CHIPS * CORES
HEADS = 4
WIDE = 2 * HD
OWN, OTHER, SEEN, SEND, LAND, CORE, DEPTHS, PAIRS, TABLE = 0, 5, 10, 14, 15, 18, 19, 24, 32
BASE = 10000.0
BF16 = jnp.bfloat16
F32 = jnp.float32

MIB = 1024 * 1024


def room(mib):
    return pltpu.CompilerParams(vmem_limit_bytes=mib * MIB)


VMEM = pl.BlockSpec(memory_space=pltpu.VMEM)
SMEM = pl.BlockSpec(memory_space=pltpu.SMEM)


def plan_kernel(gap_ref, table):
    row, chip, core = (lax.axis_index(name) for name in ("row", "chip", "core"))
    count = gap_ref.shape[0]
    first = row * ROW
    shard = first + chip * CORES + core
    pick = lambda cond, a, b: jnp.where(cond, a, b)

    def gap_of(node):
        inside = gap_ref[jnp.clip(node, 0, count - 1)]
        return pick(node >= count, 1, pick(node < 0, 0, inside))

    def elders_of(node):
        found = []
        for _ in range(LEVELS):
            gap = gap_of(node)
            node = pick(gap > 0, node - gap, -1)
            found.append(node)
        return found

    def deeper(node, depth):
        return depth + pick(gap_ref[node] == 1, 1, 0)

    depth = lax.fori_loop(0, first + chip * CORES + 1, deeper, jnp.int32(0))
    pair_depth = [depth, deeper(first + chip * CORES + 1, depth)]
    own_depth = pick(core == 0, pair_depth[0], pair_depth[1])
    stack, relay = elders_of(first), elders_of(first + ROW)
    for start, node, half in (
        (OWN, shard, core),
        (OTHER, shard + 1 - 2 * core, 1 - core),
    ):
        table[start] = half
        for i, elder in enumerate(elders_of(node)):
            in_row = 2 * (chip - ((elder - first) >> 1)) + (elder & 1)
            before = jnp.int32(0)
            for j in range(LEVELS):
                before = pick(elder == stack[j], 3 * CHIPS - 1 - j - chip, before)
            code = pick(elder < 0, 0, pick(elder >= first, in_row, before))
            table[start + 1 + i] = jnp.clip(code, 0, 3 * CHIPS - 1)
            if start == OWN:
                table[SEEN + i] = pick(elder >= 0, 1, 0)

    def held(rank):
        node = jnp.int32(-1)
        for j in range(LEVELS):
            node = pick(rank == j, relay[j], node)
        return node

    node = held(CHIPS - 1 - chip)
    code = 2 * (((node - first) >> 1) - chip) + (node & 1)
    table[SEND] = jnp.clip(code, 0, 2 * CHIPS - 3)
    for i, rank in enumerate((CHIPS - 1 - chip, CHIPS - chip, pick(chip == 2, CHIPS - 1, CHIPS))):
        node = held(rank)
        here = (node >= first) & (((node - first) >> 1) == chip)
        table[LAND + i] = pick(here, node & 1, CORES)
    table[CORE] = core
    for i in range(SLOTS):
        table[DEPTHS + i] = own_depth - i
    for i in range(CORES):
        table[PAIRS + i] = pair_depth[i]
    for i in range(PAIRS + CORES, TABLE):
        table[i] = 0


def call_plan(parent_gap):
    return pl.pallas_call(
        plan_kernel,
        out_shape=jax.ShapeDtypeStruct((TABLE,), jnp.int32),
        in_specs=[SMEM],
        out_specs=SMEM,
    )(parent_gap)


def angles_of(depth):
    frequency = jnp.exp(jnp.arange(HALF, dtype=F32) * (-2.0 * math.log(BASE) / HD))
    position = (depth[:, None] * TOK + jnp.arange(TOK, dtype=jnp.int32)[None, :]).reshape(-1)
    return position.astype(F32)[:, None] * frequency[None, :]


def turn(block, cosine, sine):
    first, second = block[:, :HALF], block[:, HALF:]
    return jnp.concatenate(
        [first * cosine - second * sine, second * cosine + first * sine], -1
    )


def fetch(code, sources, target):
    at = 0
    for ref in sources:
        for half in range(ref.shape[0] // TOK):

            @pl.when(code == at)
            def _(ref=ref, half=half):
                target[...] = ref[half * TOK : (half + 1) * TOK, :]

            at += 1


def part(ref, i):
    return ref.at[pl.ds(i * TOK, TOK)]


def pick_kernel(offset, number, table, *refs):
    sources, o_ref = refs[:-1], refs[-1]
    for i in range(number):
        fetch(table[offset + i], sources, part(o_ref, i))


def call_pick(table, sources, offset, number):
    return pl.pallas_call(
        functools.partial(pick_kernel, offset, number),
        compiler_params=room(4),
        out_shape=jax.ShapeDtypeStruct((number * TOK, HD), BF16),
        in_specs=[SMEM] + [VMEM] * len(sources),
        out_specs=VMEM,
    )(table, *sources)


NT = (((1,), (1,)), ((), ()))
NN = (((1,), (0,)), ((), ()))
TN = (((0,), (0,)), ((), ()))


def dot(a, b, dims):
    return lax.dot_general(a, b, dims, preferred_element_type=F32)


def attend_kernel(table, qg_ref, cos_ref, sin_ref, other_ref, *refs):
    sources = refs[: 2 * CHIPS]
    out_ref, keep_ref, give_ref = refs[2 * CHIPS : 2 * CHIPS + 3]
    mine_ref, keys, vals, q_all, low_all, score_all = refs[2 * CHIPS + 3 :]
    for i in range(SLOTS):
        fetch(table[OWN + i], sources, part(mine_ref, i))
    for h in range(2):
        q_all[h * TOK : (h + 1) * TOK, :] = turn(
            qg_ref[:, h * HD : (h + 1) * HD].astype(F32), cos_ref[:TOK, :], sin_ref[:TOK, :]
        ).astype(BF16)
    is_key = table[CORE] == 0
    for i in range(SLOTS):
        here = slice(i * TOK, (i + 1) * TOK)
        mine, other = mine_ref[here, :], other_ref[here, :]
        keys[here, :] = turn(
            jnp.where(is_key, mine, other).astype(F32), cos_ref[here, :], sin_ref[here, :]
        ).astype(BF16)
        vals[here, :] = jnp.where(is_key, other, mine)
    scaling = HD**-0.5
    earlier = lax.broadcasted_iota(jnp.int32, (TOK, TOK), 1) <= lax.broadcasted_iota(
        jnp.int32, (TOK, TOK), 0
    )
    last = SLOTS - 1
    block = lambda ref, i: ref[i * TOK : (i + 1) * TOK, :]
    for h in range(2):
        rows = slice(h * TOK, (h + 1) * TOK)
        q, g = q_all[rows, :], qg_ref[:, WIDE + h * HD : WIDE + (h + 1) * HD]

        def joint(a, which, fill):
            parts = [dot(a, block(which, i), NT) for i in range(SLOTS)]
            if fill is None:
                return [jnp.where(earlier, parts[0], parts[last])] + parts[1:last]
            parts = [parts[0] * scaling] + [
                jnp.where(table[SEEN + i - 1] > 0, parts[i] * scaling, fill)
                for i in range(1, SLOTS)
            ]
            return [jnp.where(earlier, parts[0], parts[last])] + parts[1:last]

        scores = joint(q, keys, -1e30)
        top = functools.reduce(jnp.maximum, scores)
        top = jnp.max(top, -1, keepdims=True)
        raw = [jnp.exp(s - top) for s in scores]
        share = 1.0 / jnp.sum(functools.reduce(jnp.add, raw), -1, keepdims=True)
        probs = [r * share for r in raw]
        grads = joint(g, vals, None)
        delta = functools.reduce(jnp.add, [p * d for p, d in zip(probs, grads)])
        delta = jnp.sum(delta, -1, keepdims=True)
        for ref, parts in (
            (low_all, probs),
            (score_all, [p * (d - delta) * scaling for p, d in zip(probs, grads)]),
        ):
            ref[rows, :TOK] = jnp.where(earlier, parts[0], 0.0).astype(BF16)
            ref[rows, last * TOK :] = jnp.where(earlier, 0.0, parts[0]).astype(BF16)
            for i in range(1, last):
                ref[rows, i * TOK : (i + 1) * TOK] = parts[i].astype(BF16)
        out_ref[:, h * HD : (h + 1) * HD] = dot(low_all[rows, :], vals[...], NN).astype(BF16)
        out_ref[:, WIDE + h * HD : WIDE + (h + 1) * HD] = turn(
            dot(score_all[rows, :], keys[...], NN), cos_ref[:TOK, :], -sin_ref[:TOK, :]
        ).astype(BF16)
    for i in range(SLOTS):
        cols = slice(i * TOK, (i + 1) * TOK)
        part_key = dot(score_all[:, cols], q_all[...], TN)
        part_value = dot(low_all[:TOK, cols], qg_ref[:, WIDE : WIDE + HD], TN) + dot(
            low_all[TOK:, cols], qg_ref[:, WIDE + HD :], TN
        )
        keep_ref[cols, :] = jnp.where(is_key, part_key, part_value).astype(BF16)
        give_ref[cols, :] = jnp.where(is_key, part_value, part_key).astype(BF16)


def call_attend(table, query_grad, cosine, sine, other, sources):
    return pl.pallas_call(
        attend_kernel,
        compiler_params=room(24),
        out_shape=(
            jax.ShapeDtypeStruct((TOK, 2 * WIDE), BF16),
            jax.ShapeDtypeStruct((KEYS, HD), BF16),
            jax.ShapeDtypeStruct((KEYS, HD), BF16),
        ),
        in_specs=[SMEM] + [VMEM] * (4 + len(sources)),
        out_specs=(VMEM,) * 3,
        scratch_shapes=[
            pltpu.VMEM((KEYS, HD), BF16),
            pltpu.VMEM((KEYS, HD), BF16),
            pltpu.VMEM((KEYS, HD), BF16),
            pltpu.VMEM((2 * TOK, HD), BF16),
            pltpu.VMEM((2 * TOK, KEYS), BF16),
            pltpu.VMEM((2 * TOK, KEYS), BF16),
        ],
    )(table, query_grad, cosine, sine, other, *sources)


def spread_kernel(table, keep_ref, got_ref, *refs):
    outs, total = refs[:-1], refs[-1]
    total[...] = jnp.zeros_like(total)
    for source, offset in ((keep_ref, OWN), (got_ref, OTHER)):
        for i in range(SLOTS):
            at = pl.ds(pl.multiple_of(table[offset + i] * TOK, TOK), TOK)
            total[at, :] += source[i * TOK : (i + 1) * TOK, :].astype(F32)
    for k in range(CHIPS):
        outs[k][...] = total[k * PAIR : (k + 1) * PAIR, :].astype(outs[k].dtype)
        low = CHIPS * PAIR + k * TOK
        outs[CHIPS + k][...] = total[low : low + TOK, :].astype(BF16)


def call_spread(table, keep, got):
    return pl.pallas_call(
        spread_kernel,
        compiler_params=room(12),
        out_shape=tuple(
            [jax.ShapeDtypeStruct((PAIR, HD), F32)]
            + [jax.ShapeDtypeStruct((PAIR, HD), BF16)] * (CHIPS - 1)
            + [jax.ShapeDtypeStruct((TOK, HD), BF16)] * CHIPS
        ),
        in_specs=[SMEM, VMEM, VMEM],
        out_specs=(VMEM,) * (2 * CHIPS),
        scratch_shapes=[
            pltpu.VMEM((CHIPS * PAIR + CHIPS * TOK, HD), F32),
        ],
    )(table, keep, got)


def sum_kernel(*refs):
    total = refs[0][...].astype(F32)
    for ref in refs[1:-1]:
        total = total + ref[...].astype(F32)
    refs[-1][...] = total.astype(refs[-1].dtype)


def call_sum(parts, dtype):
    return pl.pallas_call(
        sum_kernel,
        compiler_params=room(6),
        out_shape=jax.ShapeDtypeStruct(parts[0].shape, dtype),
        in_specs=[VMEM] * len(parts),
        out_specs=VMEM,
    )(*parts)


def close_kernel(table, own_ref, *refs):
    backs = refs[:-4]
    cos_ref, sin_ref, o_ref, total = refs[-4:]
    total[...] = own_ref[...]
    for k, back in enumerate(backs):
        code = table[LAND + k]

        @pl.when(code < CORES)
        def _(back=back, code=code):
            at = pl.ds(pl.multiple_of(code * TOK, TOK), TOK)
            total[at, :] += back[...].astype(F32)

    is_key = table[CORE] == 0

    @pl.when(is_key)
    def _():
        o_ref[...] = turn(total[...], cos_ref[...], -sin_ref[...]).astype(BF16)

    @pl.when(jnp.logical_not(is_key))
    def _():
        o_ref[...] = total[...].astype(BF16)


def call_close(table, own, backs, cosine, sine):
    return pl.pallas_call(
        close_kernel,
        compiler_params=room(8),
        out_shape=jax.ShapeDtypeStruct((PAIR, HD), BF16),
        in_specs=[SMEM] + [VMEM] * (3 + len(backs)),
        out_specs=VMEM,
        scratch_shapes=[pltpu.VMEM((PAIR, HD), F32)],
    )(table, own, *backs, cosine, sine)


def along(block, shift, starts=range(CHIPS)):
    return lax.ppermute(
        block, "chip", [(i, i + shift) for i in starts if 0 <= i + shift < CHIPS]
    )


def next_row(block, shift):
    rows = lax.axis_size("row")
    return lax.ppermute(
        block, "row", [(i, i + shift) for i in range(rows) if 0 <= i + shift < rows]
    )


def swap(block):
    return lax.ppermute(block, "core", [(0, 1), (1, 0)])


def shards(queries, keys, values, grad_attn, parent_gap):
    tokens = queries.shape[0]
    both = lax.all_to_all(
        jnp.concatenate([keys, values], 1),
        ("core", "head"),
        split_axis=1,
        concat_axis=0,
        tiled=True,
    )
    table = call_plan(parent_gap)
    slot_angles = angles_of(table[DEPTHS : DEPTHS + SLOTS])
    pair_angles = angles_of(table[PAIRS : PAIRS + CORES])
    slot_cos, slot_sin = jnp.cos(slot_angles), jnp.sin(slot_angles)
    pair_cos, pair_sin = jnp.cos(pair_angles), jnp.sin(pair_angles)
    both, slot_cos, slot_sin = lax.optimization_barrier((both, slot_cos, slot_sin))
    pairs = [both, along(both, -1), along(both, -2, (2,))]
    query_grad = jnp.concatenate(
        [queries.reshape(tokens, HEADS, WIDE), grad_attn.reshape(tokens, HEADS, WIDE)], 2
    ).reshape(tokens, HEADS * 2 * WIDE)
    query_grad = lax.all_to_all(query_grad, "head", split_axis=1, concat_axis=0, tiled=True)
    held = call_pick(table, pairs, SEND, 1)
    relay = next_row(held, 1)
    relay, query_grad, pair_cos, pair_sin = lax.optimization_barrier(
        (relay, query_grad, pair_cos, pair_sin)
    )
    sources = [both] + [along(both, k) for k in (1, 2, 3)]
    sources += [relay] + [along(relay, -k) for k in (1, 2, 3)]
    other = swap(call_pick(table, sources, OTHER, SLOTS))
    out, keep, give = call_attend(table, query_grad, slot_cos, slot_sin, other, sources)
    got = swap(give)
    out = lax.all_to_all(out, "head", split_axis=0, concat_axis=1, tiled=True)
    spread = call_spread(table, keep, got)
    own, within, stack = spread[0], spread[1:CHIPS], spread[CHIPS:]
    stack_sum = call_sum([stack[0]] + [along(stack[k], k) for k in (1, 2, 3)], BF16)
    back = next_row(stack_sum, -1)
    own = call_sum([own] + [along(within[k - 1], -k) for k in (1, 2, 3)], F32)
    backs = [back, along(back, 1), along(back, 2, (0,))]
    grad_both = call_close(table, own, backs, pair_cos, pair_sin)
    grad_both, out = lax.optimization_barrier((grad_both, out))
    grad_both = lax.all_to_all(grad_both, ("core", "head"), split_axis=0, concat_axis=1, tiled=True)
    out = out.reshape(tokens, HEADS, 2, WIDE)
    attended = out[:, :, 0].reshape(tokens, HEADS * WIDE)
    grad_query = out[:, :, 1].reshape(tokens, HEADS * WIDE)
    half = HEADS * HD
    return attended, grad_query, grad_both[:, :half], grad_both[:, half:]


def solution(mesh):
    devices = mesh.devices
    rows = devices.shape[0] // ROW
    split = Mesh(
        devices.reshape(rows, CHIPS, CORES, devices.shape[1]), ("row", "chip", "core", "head")
    )
    spec = P(("row", "chip", "core", "head"), None)

    return jax.shard_map(
        shards,
        mesh=split,
        in_specs=(spec, spec, spec, spec, P()),
        out_specs=(spec, spec, spec, spec),
        check_vma=False,
    )
```

```python
import functools
import math

import jax
import jax.numpy as jnp
from jax import lax
from jax.experimental import pallas as pl
from jax.experimental.pallas import tpu as pltpu
from jax.sharding import Mesh
from jax.sharding import PartitionSpec as P


HD = 256
HALF = HD // 2
TOK = 256
LEVELS = 4
SLOTS = LEVELS + 1
CHIPS = 4
CORES = 2
PAIR = CORES * TOK
KEYS = SLOTS * TOK
ROW = CHIPS * CORES
HEADS = 4
WIDE = 2 * HD
OWN, OTHER, SEEN, SEND, LAND, CORE, DEPTHS, PAIRS, TABLE = 0, 5, 10, 14, 15, 18, 19, 24, 32
BASE = 10000.0
BF16 = jnp.bfloat16
F32 = jnp.float32

MIB = 1024 * 1024


def room(mib):
    return pltpu.CompilerParams(vmem_limit_bytes=mib * MIB)


VMEM = pl.BlockSpec(memory_space=pltpu.VMEM)
SMEM = pl.BlockSpec(memory_space=pltpu.SMEM)


def plan_kernel(gap_ref, table):
    row, chip, core = (lax.axis_index(name) for name in ("row", "chip", "core"))
    count = gap_ref.shape[0]
    first = row * ROW
    shard = first + chip * CORES + core
    pick = lambda cond, a, b: jnp.where(cond, a, b)

    def gap_of(node):
        inside = gap_ref[jnp.clip(node, 0, count - 1)]
        return pick(node >= count, 1, pick(node < 0, 0, inside))

    def elders_of(node):
        found = []
        for _ in range(LEVELS):
            gap = gap_of(node)
            node = pick(gap > 0, node - gap, -1)
            found.append(node)
        return found

    def deeper(node, depth):
        return depth + pick(gap_ref[node] == 1, 1, 0)

    depth = lax.fori_loop(0, first + chip * CORES + 1, deeper, jnp.int32(0))
    pair_depth = [depth, deeper(first + chip * CORES + 1, depth)]
    own_depth = pick(core == 0, pair_depth[0], pair_depth[1])
    stack, relay = elders_of(first), elders_of(first + ROW)
    for start, node, half in (
        (OWN, shard, core),
        (OTHER, shard + 1 - 2 * core, 1 - core),
    ):
        table[start] = half
        for i, elder in enumerate(elders_of(node)):
            in_row = 2 * (chip - ((elder - first) >> 1)) + (elder & 1)
            before = jnp.int32(0)
            for j in range(LEVELS):
                before = pick(elder == stack[j], 3 * CHIPS - 1 - j - chip, before)
            code = pick(elder < 0, 0, pick(elder >= first, in_row, before))
            table[start + 1 + i] = jnp.clip(code, 0, 3 * CHIPS - 1)
            if start == OWN:
                table[SEEN + i] = pick(elder >= 0, 1, 0)

    def held(rank):
        node = jnp.int32(-1)
        for j in range(LEVELS):
            node = pick(rank == j, relay[j], node)
        return node

    node = held(CHIPS - 1 - chip)
    code = 2 * (((node - first) >> 1) - chip) + (node & 1)
    table[SEND] = jnp.clip(code, 0, 2 * CHIPS - 3)
    for i, rank in enumerate((CHIPS - 1 - chip, CHIPS - chip, pick(chip == 2, CHIPS - 1, CHIPS))):
        node = held(rank)
        here = (node >= first) & (((node - first) >> 1) == chip)
        table[LAND + i] = pick(here, node & 1, CORES)
    table[CORE] = core
    for i in range(SLOTS):
        table[DEPTHS + i] = own_depth - i
    for i in range(CORES):
        table[PAIRS + i] = pair_depth[i]
    for i in range(PAIRS + CORES, TABLE):
        table[i] = 0


def call_plan(parent_gap):
    return pl.pallas_call(
        plan_kernel,
        out_shape=jax.ShapeDtypeStruct((TABLE,), jnp.int32),
        in_specs=[SMEM],
        out_specs=SMEM,
    )(parent_gap)


def angles_of(depth):
    frequency = jnp.exp(jnp.arange(HALF, dtype=F32) * (-2.0 * math.log(BASE) / HD))
    position = (depth[:, None] * TOK + jnp.arange(TOK, dtype=jnp.int32)[None, :]).reshape(-1)
    return position.astype(F32)[:, None] * frequency[None, :]


def turn(block, cosine, sine):
    first, second = block[:, :HALF], block[:, HALF:]
    return jnp.concatenate(
        [first * cosine - second * sine, second * cosine + first * sine], -1
    )


def fetch(code, sources, target):
    at = 0
    for ref in sources:
        for half in range(ref.shape[0] // TOK):

            @pl.when(code == at)
            def _(ref=ref, half=half):
                target[...] = ref[half * TOK : (half + 1) * TOK, :]

            at += 1


def part(ref, i):
    return ref.at[pl.ds(i * TOK, TOK)]


def pick_kernel(offset, number, table, *refs):
    sources, o_ref = refs[:-1], refs[-1]
    for i in range(number):
        fetch(table[offset + i], sources, part(o_ref, i))


def call_pick(table, sources, offset, number):
    return pl.pallas_call(
        functools.partial(pick_kernel, offset, number),
        compiler_params=room(4),
        out_shape=jax.ShapeDtypeStruct((number * TOK, HD), BF16),
        in_specs=[SMEM] + [VMEM] * len(sources),
        out_specs=VMEM,
    )(table, *sources)


NT = (((1,), (1,)), ((), ()))
NN = (((1,), (0,)), ((), ()))
TN = (((0,), (0,)), ((), ()))


def dot(a, b, dims):
    return lax.dot_general(a, b, dims, preferred_element_type=F32)


def attend_kernel(table, qg_ref, cos_ref, sin_ref, other_ref, *refs):
    sources = refs[: 2 * CHIPS]
    out_ref, keep_ref, give_ref = refs[2 * CHIPS : 2 * CHIPS + 3]
    mine_ref, keys, vals, q_all, low_all, score_all = refs[2 * CHIPS + 3 :]
    for i in range(SLOTS):
        fetch(table[OWN + i], sources, part(mine_ref, i))
    for h in range(2):
        q_all[h * TOK : (h + 1) * TOK, :] = turn(
            qg_ref[:, h * HD : (h + 1) * HD].astype(F32), cos_ref[:TOK, :], sin_ref[:TOK, :]
        ).astype(BF16)
    is_key = table[CORE] == 0
    for i in range(SLOTS):
        here = slice(i * TOK, (i + 1) * TOK)
        mine, other = mine_ref[here, :], other_ref[here, :]
        keys[here, :] = turn(
            jnp.where(is_key, mine, other).astype(F32), cos_ref[here, :], sin_ref[here, :]
        ).astype(BF16)
        vals[here, :] = jnp.where(is_key, other, mine)
    scaling = HD**-0.5
    earlier = lax.broadcasted_iota(jnp.int32, (TOK, TOK), 1) <= lax.broadcasted_iota(
        jnp.int32, (TOK, TOK), 0
    )
    last = SLOTS - 1
    block = lambda ref, i: ref[i * TOK : (i + 1) * TOK, :]
    for h in range(2):
        rows = slice(h * TOK, (h + 1) * TOK)
        q, g = q_all[rows, :], qg_ref[:, WIDE + h * HD : WIDE + (h + 1) * HD]

        def joint(a, which, fill):
            parts = [dot(a, block(which, i), NT) for i in range(SLOTS)]
            if fill is None:
                return [jnp.where(earlier, parts[0], parts[last])] + parts[1:last]
            parts = [parts[0] * scaling] + [
                jnp.where(table[SEEN + i - 1] > 0, parts[i] * scaling, fill)
                for i in range(1, SLOTS)
            ]
            return [jnp.where(earlier, parts[0], parts[last])] + parts[1:last]

        scores = joint(q, keys, -1e30)
        top = functools.reduce(jnp.maximum, scores)
        top = jnp.max(top, -1, keepdims=True)
        raw = [jnp.exp(s - top) for s in scores]
        share = 1.0 / jnp.sum(functools.reduce(jnp.add, raw), -1, keepdims=True)
        probs = [r * share for r in raw]
        grads = joint(g, vals, None)
        delta = functools.reduce(jnp.add, [p * d for p, d in zip(probs, grads)])
        delta = jnp.sum(delta, -1, keepdims=True)
        for ref, parts in (
            (low_all, probs),
            (score_all, [p * (d - delta) * scaling for p, d in zip(probs, grads)]),
        ):
            ref[rows, :TOK] = jnp.where(earlier, parts[0], 0.0).astype(BF16)
            ref[rows, last * TOK :] = jnp.where(earlier, 0.0, parts[0]).astype(BF16)
            for i in range(1, last):
                ref[rows, i * TOK : (i + 1) * TOK] = parts[i].astype(BF16)
        out_ref[:, h * HD : (h + 1) * HD] = dot(low_all[rows, :], vals[...], NN).astype(BF16)
        out_ref[:, WIDE + h * HD : WIDE + (h + 1) * HD] = turn(
            dot(score_all[rows, :], keys[...], NN), cos_ref[:TOK, :], -sin_ref[:TOK, :]
        ).astype(BF16)
    for i in range(SLOTS):
        cols = slice(i * TOK, (i + 1) * TOK)
        part_key = dot(score_all[:, cols], q_all[...], TN)
        part_value = dot(low_all[:TOK, cols], qg_ref[:, WIDE : WIDE + HD], TN) + dot(
            low_all[TOK:, cols], qg_ref[:, WIDE + HD :], TN
        )
        keep_ref[cols, :] = jnp.where(is_key, part_key, part_value).astype(BF16)
        give_ref[cols, :] = jnp.where(is_key, part_value, part_key).astype(BF16)


def call_attend(table, query_grad, cosine, sine, other, sources):
    return pl.pallas_call(
        attend_kernel,
        compiler_params=room(24),
        out_shape=(
            jax.ShapeDtypeStruct((TOK, 2 * WIDE), BF16),
            jax.ShapeDtypeStruct((KEYS, HD), BF16),
            jax.ShapeDtypeStruct((KEYS, HD), BF16),
        ),
        in_specs=[SMEM] + [VMEM] * (4 + len(sources)),
        out_specs=(VMEM,) * 3,
        scratch_shapes=[
            pltpu.VMEM((KEYS, HD), BF16),
            pltpu.VMEM((KEYS, HD), BF16),
            pltpu.VMEM((KEYS, HD), BF16),
            pltpu.VMEM((2 * TOK, HD), BF16),
            pltpu.VMEM((2 * TOK, KEYS), BF16),
            pltpu.VMEM((2 * TOK, KEYS), BF16),
        ],
    )(table, query_grad, cosine, sine, other, *sources)


def spread_kernel(table, keep_ref, got_ref, *refs):
    outs, total = refs[:-1], refs[-1]
    total[...] = jnp.zeros_like(total)
    for source, offset in ((keep_ref, OWN), (got_ref, OTHER)):
        for i in range(SLOTS):
            at = pl.ds(pl.multiple_of(table[offset + i] * TOK, TOK), TOK)
            total[at, :] += source[i * TOK : (i + 1) * TOK, :].astype(F32)
    for k in range(CHIPS):
        outs[k][...] = total[k * PAIR : (k + 1) * PAIR, :].astype(outs[k].dtype)
        low = CHIPS * PAIR + k * TOK
        outs[CHIPS + k][...] = total[low : low + TOK, :].astype(BF16)


def call_spread(table, keep, got):
    return pl.pallas_call(
        spread_kernel,
        compiler_params=room(12),
        out_shape=tuple(
            [jax.ShapeDtypeStruct((PAIR, HD), F32)]
            + [jax.ShapeDtypeStruct((PAIR, HD), BF16)] * (CHIPS - 1)
            + [jax.ShapeDtypeStruct((TOK, HD), BF16)] * CHIPS
        ),
        in_specs=[SMEM, VMEM, VMEM],
        out_specs=(VMEM,) * (2 * CHIPS),
        scratch_shapes=[
            pltpu.VMEM((CHIPS * PAIR + CHIPS * TOK, HD), F32),
        ],
    )(table, keep, got)


def sum_kernel(*refs):
    total = refs[0][...].astype(F32)
    for ref in refs[1:-1]:
        total = total + ref[...].astype(F32)
    refs[-1][...] = total.astype(refs[-1].dtype)


def call_sum(parts, dtype):
    return pl.pallas_call(
        sum_kernel,
        compiler_params=room(6),
        out_shape=jax.ShapeDtypeStruct(parts[0].shape, dtype),
        in_specs=[VMEM] * len(parts),
        out_specs=VMEM,
    )(*parts)


def close_kernel(table, own_ref, *refs):
    backs = refs[:-4]
    cos_ref, sin_ref, o_ref, total = refs[-4:]
    total[...] = own_ref[...]
    for k, back in enumerate(backs):
        code = table[LAND + k]

        @pl.when(code < CORES)
        def _(back=back, code=code):
            at = pl.ds(pl.multiple_of(code * TOK, TOK), TOK)
            total[at, :] += back[...].astype(F32)

    is_key = table[CORE] == 0

    @pl.when(is_key)
    def _():
        o_ref[...] = turn(total[...], cos_ref[...], -sin_ref[...]).astype(BF16)

    @pl.when(jnp.logical_not(is_key))
    def _():
        o_ref[...] = total[...].astype(BF16)


def call_close(table, own, backs, cosine, sine):
    return pl.pallas_call(
        close_kernel,
        compiler_params=room(8),
        out_shape=jax.ShapeDtypeStruct((PAIR, HD), BF16),
        in_specs=[SMEM] + [VMEM] * (3 + len(backs)),
        out_specs=VMEM,
        scratch_shapes=[pltpu.VMEM((PAIR, HD), F32)],
    )(table, own, *backs, cosine, sine)


def along(block, shift, starts=range(CHIPS)):
    return lax.ppermute(
        block, "chip", [(i, i + shift) for i in starts if 0 <= i + shift < CHIPS]
    )


def next_row(block, shift):
    rows = lax.axis_size("row")
    return lax.ppermute(
        block, "row", [(i, i + shift) for i in range(rows) if 0 <= i + shift < rows]
    )


def swap(block):
    return lax.ppermute(block, "core", [(0, 1), (1, 0)])


def shards(queries, keys, values, grad_attn, parent_gap):
    tokens = queries.shape[0]
    chunks = [
        x.reshape(tokens, HEADS, HD).transpose(1, 0, 2) for x in (keys, values)
    ]
    both = lax.all_to_all(
        jnp.concatenate(chunks, 0), ("core", "head"), split_axis=0, concat_axis=0, tiled=True
    ).reshape(PAIR, HD)
    table = call_plan(parent_gap)
    slot_angles = angles_of(table[DEPTHS : DEPTHS + SLOTS])
    pair_angles = angles_of(table[PAIRS : PAIRS + CORES])
    slot_cos, slot_sin = jnp.cos(slot_angles), jnp.sin(slot_angles)
    pair_cos, pair_sin = jnp.cos(pair_angles), jnp.sin(pair_angles)
    both, slot_cos, slot_sin = lax.optimization_barrier((both, slot_cos, slot_sin))
    pairs = [both, along(both, -1), along(both, -2, (2,))]
    query_grad = jnp.concatenate(
        [queries.reshape(tokens, HEADS, WIDE), grad_attn.reshape(tokens, HEADS, WIDE)], 2
    ).reshape(tokens, HEADS * 2 * WIDE)
    query_grad = lax.all_to_all(query_grad, "head", split_axis=1, concat_axis=0, tiled=True)
    held = call_pick(table, pairs, SEND, 1)
    relay = next_row(held, 1)
    relay, query_grad = lax.optimization_barrier((relay, query_grad))
    sources = [both] + [along(both, k) for k in (1, 2, 3)]
    sources += [relay] + [along(relay, -k) for k in (1, 2, 3)]
    other = swap(call_pick(table, sources, OTHER, SLOTS))
    out, keep, give = call_attend(table, query_grad, slot_cos, slot_sin, other, sources)
    got = swap(give)
    out = lax.all_to_all(out, "head", split_axis=0, concat_axis=1, tiled=True)
    spread = call_spread(table, keep, got)
    own, within, stack = spread[0], spread[1:CHIPS], spread[CHIPS:]
    stack_sum = call_sum([stack[0]] + [along(stack[k], k) for k in (1, 2, 3)], BF16)
    back = next_row(stack_sum, -1)
    back, pair_cos, pair_sin = lax.optimization_barrier((back, pair_cos, pair_sin))
    own = call_sum([own] + [along(within[k - 1], -k) for k in (1, 2, 3)], F32)
    backs = [back, along(back, 1), along(back, 2, (0,))]
    grad_both = call_close(table, own, backs, pair_cos, pair_sin)
    grad_both, out = lax.optimization_barrier((grad_both, out))
    grad_both = lax.all_to_all(grad_both, ("core", "head"), split_axis=0, concat_axis=1, tiled=True)
    out = out.reshape(tokens, HEADS, 2, WIDE)
    attended = out[:, :, 0].reshape(tokens, HEADS * WIDE)
    grad_query = out[:, :, 1].reshape(tokens, HEADS * WIDE)
    half = HEADS * HD
    return attended, grad_query, grad_both[:, :half], grad_both[:, half:]


def solution(mesh):
    devices = mesh.devices
    rows = devices.shape[0] // ROW
    split = Mesh(
        devices.reshape(rows, CHIPS, CORES, devices.shape[1]), ("row", "chip", "core", "head")
    )
    spec = P(("row", "chip", "core", "head"), None)

    return jax.shard_map(
        shards,
        mesh=split,
        in_specs=(spec, spec, spec, spec, P()),
        out_specs=(spec, spec, spec, spec),
        check_vma=False,
    )
```

```python
import functools
import math

import jax
import jax.numpy as jnp
from jax import lax
from jax.experimental import pallas as pl
from jax.experimental.pallas import tpu as pltpu
from jax.sharding import Mesh
from jax.sharding import PartitionSpec as P


HD = 256
HALF = HD // 2
TOK = 256
LEVELS = 4
SLOTS = LEVELS + 1
CHIPS = 4
CORES = 2
PAIR = CORES * TOK
KEYS = SLOTS * TOK
ROW = CHIPS * CORES
HEADS = 4
WIDE = 2 * HD
OWN, OTHER, SEEN, SEND, LAND, CORE, DEPTHS, PAIRS, GIVE, TABLE = 0, 5, 10, 14, 15, 18, 19, 24, 26, 32
BASE = 10000.0
BF16 = jnp.bfloat16
F32 = jnp.float32

MIB = 1024 * 1024


def room(mib):
    return pltpu.CompilerParams(vmem_limit_bytes=mib * MIB)


VMEM = pl.BlockSpec(memory_space=pltpu.VMEM)
SMEM = pl.BlockSpec(memory_space=pltpu.SMEM)


def plan_kernel(gap_ref, table):
    row, chip, core = (lax.axis_index(name) for name in ("row", "chip", "core"))
    count = gap_ref.shape[0]
    first = row * ROW
    shard = first + chip * CORES + core
    pick = lambda cond, a, b: jnp.where(cond, a, b)

    def gap_of(node):
        inside = gap_ref[jnp.clip(node, 0, count - 1)]
        return pick(node >= count, 1, pick(node < 0, 0, inside))

    def elders_of(node):
        found = []
        for _ in range(LEVELS):
            gap = gap_of(node)
            node = pick(gap > 0, node - gap, -1)
            found.append(node)
        return found

    def deeper(node, depth):
        return depth + pick(gap_ref[node] == 1, 1, 0)

    depth = lax.fori_loop(0, first + chip * CORES + 1, deeper, jnp.int32(0))
    pair_depth = [depth, deeper(first + chip * CORES + 1, depth)]
    own_depth = pick(core == 0, pair_depth[0], pair_depth[1])
    stack, relay = elders_of(first), elders_of(first + ROW)
    for start, node, half in (
        (OWN, shard, core),
        (OTHER, shard + 1 - 2 * core, 1 - core),
    ):
        table[start] = half
        for i, elder in enumerate(elders_of(node)):
            in_row = 2 * (chip - ((elder - first) >> 1)) + (elder & 1)
            before = jnp.int32(0)
            for j in range(LEVELS):
                before = pick(elder == stack[j], 3 * CHIPS - 1 - j - chip, before)
            code = pick(elder < 0, 0, pick(elder >= first, in_row, before))
            table[start + 1 + i] = jnp.clip(code, 0, 3 * CHIPS - 1)
            if start == OWN:
                table[SEEN + i] = pick(elder >= 0, 1, 0)

    def held(rank):
        node = jnp.int32(-1)
        for j in range(LEVELS):
            node = pick(rank == j, relay[j], node)
        return node

    table[GIVE] = jnp.maximum(held(CHIPS - chip), 0) & 1
    table[GIVE + 1] = jnp.maximum(relay[LEVELS - 1], 0) & 1
    node = held(CHIPS - 1 - chip)
    far = ((node - first) >> 1) - chip
    table[SEND] = jnp.clip(pick(far <= 0, node & 1, 1 + far), 0, CHIPS - 1)
    for i, rank in enumerate((CHIPS - 1 - chip, CHIPS - chip, pick(chip == 2, CHIPS - 1, CHIPS))):
        node = held(rank)
        here = (node >= first) & (((node - first) >> 1) == chip)
        table[LAND + i] = pick(here, node & 1, CORES)
    table[CORE] = core
    for i in range(SLOTS):
        table[DEPTHS + i] = own_depth - i
    for i in range(CORES):
        table[PAIRS + i] = pair_depth[i]
    for i in range(GIVE + 2, TABLE):
        table[i] = 0


def call_plan(parent_gap):
    return pl.pallas_call(
        plan_kernel,
        out_shape=jax.ShapeDtypeStruct((TABLE,), jnp.int32),
        in_specs=[SMEM],
        out_specs=SMEM,
    )(parent_gap)


def angles_of(depth):
    frequency = jnp.exp(jnp.arange(HALF, dtype=F32) * (-2.0 * math.log(BASE) / HD))
    position = (depth[:, None] * TOK + jnp.arange(TOK, dtype=jnp.int32)[None, :]).reshape(-1)
    return position.astype(F32)[:, None] * frequency[None, :]


def turn(block, cosine, sine):
    first, second = block[:, :HALF], block[:, HALF:]
    return jnp.concatenate(
        [first * cosine - second * sine, second * cosine + first * sine], -1
    )


def fetch(code, sources, target):
    at = 0
    for ref in sources:
        for half in range(ref.shape[0] // TOK):

            @pl.when(code == at)
            def _(ref=ref, half=half):
                target[...] = ref[half * TOK : (half + 1) * TOK, :]

            at += 1


def part(ref, i):
    return ref.at[pl.ds(i * TOK, TOK)]


def pick_kernel(offset, number, table, *refs):
    sources, o_ref = refs[:-1], refs[-1]
    for i in range(number):
        fetch(table[offset + i], sources, part(o_ref, i))


def give_kernel(table, pair, *outs):
    for i, out in enumerate(outs):
        fetch(table[GIVE + i], (pair,), out)


def call_give(table, pair):
    return pl.pallas_call(
        give_kernel,
        compiler_params=room(4),
        out_shape=(jax.ShapeDtypeStruct((TOK, HD), BF16),) * 2,
        in_specs=[SMEM, VMEM],
        out_specs=(VMEM,) * 2,
    )(table, pair)


def call_pick(table, sources, offset, number):
    return pl.pallas_call(
        functools.partial(pick_kernel, offset, number),
        compiler_params=room(4),
        out_shape=jax.ShapeDtypeStruct((number * TOK, HD), BF16),
        in_specs=[SMEM] + [VMEM] * len(sources),
        out_specs=VMEM,
    )(table, *sources)


NT = (((1,), (1,)), ((), ()))
NN = (((1,), (0,)), ((), ()))
TN = (((0,), (0,)), ((), ()))


def dot(a, b, dims):
    return lax.dot_general(a, b, dims, preferred_element_type=F32)


def attend_kernel(table, qg_ref, cos_ref, sin_ref, other_ref, *refs):
    sources = refs[: 2 * CHIPS]
    out_ref, keep_ref, give_ref = refs[2 * CHIPS : 2 * CHIPS + 3]
    mine_ref, keys, vals, q_all, low_all, score_all = refs[2 * CHIPS + 3 :]
    for i in range(SLOTS):
        fetch(table[OWN + i], sources, part(mine_ref, i))
    for h in range(2):
        q_all[h * TOK : (h + 1) * TOK, :] = turn(
            qg_ref[:, h * HD : (h + 1) * HD].astype(F32), cos_ref[:TOK, :], sin_ref[:TOK, :]
        ).astype(BF16)
    is_key = table[CORE] == 0
    for i in range(SLOTS):
        here = slice(i * TOK, (i + 1) * TOK)
        mine, other = mine_ref[here, :], other_ref[here, :]
        keys[here, :] = turn(
            jnp.where(is_key, mine, other).astype(F32), cos_ref[here, :], sin_ref[here, :]
        ).astype(BF16)
        vals[here, :] = jnp.where(is_key, other, mine)
    scaling = HD**-0.5
    earlier = lax.broadcasted_iota(jnp.int32, (TOK, TOK), 1) <= lax.broadcasted_iota(
        jnp.int32, (TOK, TOK), 0
    )
    last = SLOTS - 1
    block = lambda ref, i: ref[i * TOK : (i + 1) * TOK, :]
    for h in range(2):
        rows = slice(h * TOK, (h + 1) * TOK)
        q, g = q_all[rows, :], qg_ref[:, WIDE + h * HD : WIDE + (h + 1) * HD]

        def joint(a, which, fill):
            parts = [dot(a, block(which, i), NT) for i in range(SLOTS)]
            if fill is None:
                return [jnp.where(earlier, parts[0], parts[last])] + parts[1:last]
            parts = [parts[0] * scaling] + [
                jnp.where(table[SEEN + i - 1] > 0, parts[i] * scaling, fill)
                for i in range(1, SLOTS)
            ]
            return [jnp.where(earlier, parts[0], parts[last])] + parts[1:last]

        scores = joint(q, keys, -1e30)
        top = functools.reduce(jnp.maximum, scores)
        top = jnp.max(top, -1, keepdims=True)
        raw = [jnp.exp(s - top) for s in scores]
        share = 1.0 / jnp.sum(functools.reduce(jnp.add, raw), -1, keepdims=True)
        probs = [r * share for r in raw]
        grads = joint(g, vals, None)
        delta = functools.reduce(jnp.add, [p * d for p, d in zip(probs, grads)])
        delta = jnp.sum(delta, -1, keepdims=True)
        for ref, parts in (
            (low_all, probs),
            (score_all, [p * (d - delta) * scaling for p, d in zip(probs, grads)]),
        ):
            ref[rows, :TOK] = jnp.where(earlier, parts[0], 0.0).astype(BF16)
            ref[rows, last * TOK :] = jnp.where(earlier, 0.0, parts[0]).astype(BF16)
            for i in range(1, last):
                ref[rows, i * TOK : (i + 1) * TOK] = parts[i].astype(BF16)
        out_ref[:, h * HD : (h + 1) * HD] = dot(low_all[rows, :], vals[...], NN).astype(BF16)
        out_ref[:, WIDE + h * HD : WIDE + (h + 1) * HD] = turn(
            dot(score_all[rows, :], keys[...], NN), cos_ref[:TOK, :], -sin_ref[:TOK, :]
        ).astype(BF16)
    for i in range(SLOTS):
        cols = slice(i * TOK, (i + 1) * TOK)
        part_key = dot(score_all[:, cols], q_all[...], TN)
        part_value = dot(low_all[:TOK, cols], qg_ref[:, WIDE : WIDE + HD], TN) + dot(
            low_all[TOK:, cols], qg_ref[:, WIDE + HD :], TN
        )
        keep_ref[cols, :] = jnp.where(is_key, part_key, part_value).astype(BF16)
        give_ref[cols, :] = jnp.where(is_key, part_value, part_key).astype(BF16)


def call_attend(table, query_grad, cosine, sine, other, sources):
    return pl.pallas_call(
        attend_kernel,
        compiler_params=room(24),
        out_shape=(
            jax.ShapeDtypeStruct((TOK, 2 * WIDE), BF16),
            jax.ShapeDtypeStruct((KEYS, HD), BF16),
            jax.ShapeDtypeStruct((KEYS, HD), BF16),
        ),
        in_specs=[SMEM] + [VMEM] * (4 + len(sources)),
        out_specs=(VMEM,) * 3,
        scratch_shapes=[
            pltpu.VMEM((KEYS, HD), BF16),
            pltpu.VMEM((KEYS, HD), BF16),
            pltpu.VMEM((KEYS, HD), BF16),
            pltpu.VMEM((2 * TOK, HD), BF16),
            pltpu.VMEM((2 * TOK, KEYS), BF16),
            pltpu.VMEM((2 * TOK, KEYS), BF16),
        ],
    )(table, query_grad, cosine, sine, other, *sources)


def spread_kernel(table, keep_ref, got_ref, *refs):
    outs, total = refs[:-1], refs[-1]
    total[...] = jnp.zeros_like(total)
    for source, offset in ((keep_ref, OWN), (got_ref, OTHER)):
        for i in range(SLOTS):
            at = pl.ds(pl.multiple_of(table[offset + i] * TOK, TOK), TOK)
            total[at, :] += source[i * TOK : (i + 1) * TOK, :].astype(F32)
    for k in range(CHIPS):
        outs[k][...] = total[k * PAIR : (k + 1) * PAIR, :].astype(outs[k].dtype)
        low = CHIPS * PAIR + k * TOK
        outs[CHIPS + k][...] = total[low : low + TOK, :].astype(BF16)


def call_spread(table, keep, got):
    return pl.pallas_call(
        spread_kernel,
        compiler_params=room(12),
        out_shape=tuple(
            [jax.ShapeDtypeStruct((PAIR, HD), F32)]
            + [jax.ShapeDtypeStruct((PAIR, HD), BF16)] * (CHIPS - 1)
            + [jax.ShapeDtypeStruct((TOK, HD), BF16)] * CHIPS
        ),
        in_specs=[SMEM, VMEM, VMEM],
        out_specs=(VMEM,) * (2 * CHIPS),
        scratch_shapes=[
            pltpu.VMEM((CHIPS * PAIR + CHIPS * TOK, HD), F32),
        ],
    )(table, keep, got)


def sum_kernel(*refs):
    total = refs[0][...].astype(F32)
    for ref in refs[1:-1]:
        total = total + ref[...].astype(F32)
    refs[-1][...] = total.astype(refs[-1].dtype)


def call_sum(parts, dtype):
    return pl.pallas_call(
        sum_kernel,
        compiler_params=room(6),
        out_shape=jax.ShapeDtypeStruct(parts[0].shape, dtype),
        in_specs=[VMEM] * len(parts),
        out_specs=VMEM,
    )(*parts)


def close_kernel(table, own_ref, *refs):
    backs = refs[:-4]
    cos_ref, sin_ref, o_ref, total = refs[-4:]
    total[...] = own_ref[...]
    for k, back in enumerate(backs):
        code = table[LAND + k]

        @pl.when(code < CORES)
        def _(back=back, code=code):
            at = pl.ds(pl.multiple_of(code * TOK, TOK), TOK)
            total[at, :] += back[...].astype(F32)

    is_key = table[CORE] == 0

    @pl.when(is_key)
    def _():
        o_ref[...] = turn(total[...], cos_ref[...], -sin_ref[...]).astype(BF16)

    @pl.when(jnp.logical_not(is_key))
    def _():
        o_ref[...] = total[...].astype(BF16)


def call_close(table, own, backs, cosine, sine):
    return pl.pallas_call(
        close_kernel,
        compiler_params=room(8),
        out_shape=jax.ShapeDtypeStruct((PAIR, HD), BF16),
        in_specs=[SMEM] + [VMEM] * (3 + len(backs)),
        out_specs=VMEM,
        scratch_shapes=[pltpu.VMEM((PAIR, HD), F32)],
    )(table, own, *backs, cosine, sine)


def along(block, shift, starts=range(CHIPS)):
    return lax.ppermute(block, "chip", [(i, i + shift) for i in starts if 0 <= i + shift < CHIPS])


def next_row(block, shift):
    rows = lax.axis_size("row")
    return lax.ppermute(
        block, "row", [(i, i + shift) for i in range(rows) if 0 <= i + shift < rows]
    )


def swap(block):
    return lax.ppermute(block, "core", [(0, 1), (1, 0)])


def shards(queries, keys, values, grad_attn, parent_gap):
    tokens = queries.shape[0]
    chunks = [
        x.reshape(tokens, HEADS, HD).transpose(1, 0, 2) for x in (keys, values)
    ]
    both = lax.all_to_all(
        jnp.concatenate(chunks, 0), ("core", "head"), split_axis=0, concat_axis=0, tiled=True
    ).reshape(PAIR, HD)
    table = call_plan(parent_gap)
    slot_angles = angles_of(table[DEPTHS : DEPTHS + SLOTS])
    slot_cos, slot_sin = jnp.cos(slot_angles), jnp.sin(slot_angles)
    both, slot_cos, slot_sin = lax.optimization_barrier((both, slot_cos, slot_sin))
    near, far = call_give(table, both)
    pairs = [both, along(near, -1), along(far, -2, (2,))]
    query_grad = jnp.concatenate(
        [queries.reshape(tokens, HEADS, WIDE), grad_attn.reshape(tokens, HEADS, WIDE)], 2
    ).reshape(tokens, HEADS * 2 * WIDE)
    query_grad = lax.all_to_all(query_grad, "head", split_axis=1, concat_axis=0, tiled=True)
    held = call_pick(table, pairs, SEND, 1)
    relay = next_row(held, 1)
    relay, query_grad = lax.optimization_barrier((relay, query_grad))
    sources = [both] + [along(both, k) for k in (1, 2, 3)]
    sources += [relay] + [along(relay, -k) for k in (1, 2, 3)]
    other = swap(call_pick(table, sources, OTHER, SLOTS))
    out, keep, give = call_attend(table, query_grad, slot_cos, slot_sin, other, sources)
    got = swap(give)
    out = lax.all_to_all(out, "head", split_axis=0, concat_axis=1, tiled=True)
    spread = call_spread(table, keep, got)
    own, within, stack = spread[0], spread[1:CHIPS], spread[CHIPS:]
    stack_sum = call_sum([stack[0]] + [along(stack[k], k) for k in (1, 2, 3)], BF16)
    stack_sum, late_table = lax.optimization_barrier((stack_sum, table))
    back = next_row(stack_sum, -1)
    pair_angles = angles_of(late_table[PAIRS : PAIRS + CORES])
    pair_cos, pair_sin = jnp.cos(pair_angles), jnp.sin(pair_angles)
    back, pair_cos, pair_sin = lax.optimization_barrier((back, pair_cos, pair_sin))
    own = call_sum([own] + [along(within[k - 1], -k) for k in (1, 2, 3)], F32)
    backs = [back, along(back, 1), along(back, 2, (0,))]
    grad_both = call_close(table, own, backs, pair_cos, pair_sin)
    grad_both, out = lax.optimization_barrier((grad_both, out))
    grad_both = lax.all_to_all(grad_both, ("core", "head"), split_axis=0, concat_axis=1, tiled=True)
    out = out.reshape(tokens, HEADS, 2, WIDE)
    attended = out[:, :, 0].reshape(tokens, HEADS * WIDE)
    grad_query = out[:, :, 1].reshape(tokens, HEADS * WIDE)
    half = HEADS * HD
    return attended, grad_query, grad_both[:, :half], grad_both[:, half:]


def solution(mesh):
    devices = mesh.devices
    rows = devices.shape[0] // ROW
    split = Mesh(
        devices.reshape(rows, CHIPS, CORES, devices.shape[1]), ("row", "chip", "core", "head")
    )
    spec = P(("row", "chip", "core", "head"), None)

    return jax.shard_map(
        shards,
        mesh=split,
        in_specs=(spec, spec, spec, spec, P()),
        out_specs=(spec, spec, spec, spec),
        check_vma=False,
    )
```

```python
import functools
import math

import jax
import jax.numpy as jnp
from jax import lax
from jax.experimental import pallas as pl
from jax.experimental.pallas import tpu as pltpu
from jax.sharding import Mesh
from jax.sharding import PartitionSpec as P


HD = 256
HALF = HD // 2
TOK = 256
LEVELS = 4
SLOTS = LEVELS + 1
CHIPS = 4
CORES = 2
PAIR = CORES * TOK
KEYS = SLOTS * TOK
ROW = CHIPS * CORES
HEADS = 4
WIDE = 2 * HD
OWN, OTHER, SEEN, SEND, LAND, CORE, DEPTHS, PAIRS, GIVE, TABLE = 0, 5, 10, 14, 15, 18, 19, 24, 26, 32
BASE = 10000.0
BF16 = jnp.bfloat16
F32 = jnp.float32

MIB = 1024 * 1024


def room(mib):
    return pltpu.CompilerParams(vmem_limit_bytes=mib * MIB)


VMEM = pl.BlockSpec(memory_space=pltpu.VMEM)
SMEM = pl.BlockSpec(memory_space=pltpu.SMEM)


def plan_kernel(gap_ref, table):
    row, chip, core = (lax.axis_index(name) for name in ("row", "chip", "core"))
    count = gap_ref.shape[0]
    first = row * ROW
    shard = first + chip * CORES + core
    pick = lambda cond, a, b: jnp.where(cond, a, b)

    def gap_of(node):
        inside = gap_ref[jnp.clip(node, 0, count - 1)]
        return pick(node >= count, 1, pick(node < 0, 0, inside))

    def elders_of(node):
        found = []
        for _ in range(LEVELS):
            gap = gap_of(node)
            node = pick(gap > 0, node - gap, -1)
            found.append(node)
        return found

    def deeper(node, depth):
        return depth + pick(gap_ref[node] == 1, 1, 0)

    depth = lax.fori_loop(0, first + chip * CORES + 1, deeper, jnp.int32(0))
    pair_depth = [depth, deeper(first + chip * CORES + 1, depth)]
    own_depth = pick(core == 0, pair_depth[0], pair_depth[1])
    stack, relay = elders_of(first), elders_of(first + ROW)
    for start, node, half in (
        (OWN, shard, core),
        (OTHER, shard + 1 - 2 * core, 1 - core),
    ):
        table[start] = half
        for i, elder in enumerate(elders_of(node)):
            in_row = 2 * (chip - ((elder - first) >> 1)) + (elder & 1)
            before = jnp.int32(0)
            for j in range(LEVELS):
                before = pick(elder == stack[j], 3 * CHIPS - 1 - j - chip, before)
            code = pick(elder < 0, 0, pick(elder >= first, in_row, before))
            table[start + 1 + i] = jnp.clip(code, 0, 3 * CHIPS - 1)
            if start == OWN:
                table[SEEN + i] = pick(elder >= 0, 1, 0)

    def held(rank):
        node = jnp.int32(-1)
        for j in range(LEVELS):
            node = pick(rank == j, relay[j], node)
        return node

    table[GIVE] = jnp.maximum(held(CHIPS - chip), 0) & 1
    table[GIVE + 1] = jnp.maximum(relay[LEVELS - 1], 0) & 1
    node = held(CHIPS - 1 - chip)
    far = ((node - first) >> 1) - chip
    table[SEND] = jnp.clip(pick(far <= 0, node & 1, 1 + far), 0, CHIPS - 1)
    for i, rank in enumerate((CHIPS - 1 - chip, CHIPS - chip, pick(chip == 2, CHIPS - 1, CHIPS))):
        node = held(rank)
        here = (node >= first) & (((node - first) >> 1) == chip)
        table[LAND + i] = pick(here, node & 1, CORES)
    table[CORE] = core
    for i in range(SLOTS):
        table[DEPTHS + i] = own_depth - i
    for i in range(CORES):
        table[PAIRS + i] = pair_depth[i]
    for i in range(GIVE + 2, TABLE):
        table[i] = 0


def call_plan(parent_gap):
    return pl.pallas_call(
        plan_kernel,
        out_shape=jax.ShapeDtypeStruct((TABLE,), jnp.int32),
        in_specs=[SMEM],
        out_specs=SMEM,
    )(parent_gap)


def angles_of(depth):
    frequency = jnp.exp(jnp.arange(HALF, dtype=F32) * (-2.0 * math.log(BASE) / HD))
    position = (depth[:, None] * TOK + jnp.arange(TOK, dtype=jnp.int32)[None, :]).reshape(-1)
    return position.astype(F32)[:, None] * frequency[None, :]


def turn(block, cosine, sine):
    first, second = block[:, :HALF], block[:, HALF:]
    return jnp.concatenate(
        [first * cosine - second * sine, second * cosine + first * sine], -1
    )


def fetch(code, sources, target):
    at = 0
    for ref in sources:
        for half in range(ref.shape[0] // TOK):

            @pl.when(code == at)
            def _(ref=ref, half=half):
                target[...] = ref[half * TOK : (half + 1) * TOK, :]

            at += 1


def part(ref, i):
    return ref.at[pl.ds(i * TOK, TOK)]


def pick_kernel(offset, number, table, *refs):
    sources, o_ref = refs[:-1], refs[-1]
    for i in range(number):
        fetch(table[offset + i], sources, part(o_ref, i))


def give_kernel(table, pair, *outs):
    for i, out in enumerate(outs):
        fetch(table[GIVE + i], (pair,), out)


def call_give(table, pair):
    return pl.pallas_call(
        give_kernel,
        compiler_params=room(4),
        out_shape=(jax.ShapeDtypeStruct((TOK, HD), BF16),) * 2,
        in_specs=[SMEM, VMEM],
        out_specs=(VMEM,) * 2,
    )(table, pair)


def call_pick(table, sources, offset, number):
    return pl.pallas_call(
        functools.partial(pick_kernel, offset, number),
        compiler_params=room(4),
        out_shape=jax.ShapeDtypeStruct((number * TOK, HD), BF16),
        in_specs=[SMEM] + [VMEM] * len(sources),
        out_specs=VMEM,
    )(table, *sources)


NT = (((1,), (1,)), ((), ()))
NN = (((1,), (0,)), ((), ()))
TN = (((0,), (0,)), ((), ()))


def dot(a, b, dims):
    return lax.dot_general(a, b, dims, preferred_element_type=F32)


def attend_kernel(table, qg_ref, cos_ref, sin_ref, other_ref, *refs):
    sources = refs[: 2 * CHIPS]
    out_ref, keep_ref, give_ref = refs[2 * CHIPS : 2 * CHIPS + 3]
    mine_ref, keys, vals, q_all, low_all, score_all = refs[2 * CHIPS + 3 :]
    for i in range(SLOTS):
        fetch(table[OWN + i], sources, part(mine_ref, i))
    for h in range(2):
        q_all[h * TOK : (h + 1) * TOK, :] = turn(
            qg_ref[:, h * HD : (h + 1) * HD].astype(F32), cos_ref[:TOK, :], sin_ref[:TOK, :]
        ).astype(BF16)
    is_key = table[CORE] == 0
    for i in range(SLOTS):
        here = slice(i * TOK, (i + 1) * TOK)
        mine, other = mine_ref[here, :], other_ref[here, :]
        keys[here, :] = turn(
            jnp.where(is_key, mine, other).astype(F32), cos_ref[here, :], sin_ref[here, :]
        ).astype(BF16)
        vals[here, :] = jnp.where(is_key, other, mine)
    scaling = HD**-0.5
    earlier = lax.broadcasted_iota(jnp.int32, (TOK, TOK), 1) <= lax.broadcasted_iota(
        jnp.int32, (TOK, TOK), 0
    )
    last = SLOTS - 1
    block = lambda ref, i: ref[i * TOK : (i + 1) * TOK, :]
    for h in range(2):
        rows = slice(h * TOK, (h + 1) * TOK)
        q, g = q_all[rows, :], qg_ref[:, WIDE + h * HD : WIDE + (h + 1) * HD]

        def joint(a, which, fill):
            parts = [dot(a, block(which, i), NT) for i in range(SLOTS)]
            if fill is None:
                return [jnp.where(earlier, parts[0], parts[last])] + parts[1:last]
            parts = [parts[0] * scaling] + [
                jnp.where(table[SEEN + i - 1] > 0, parts[i] * scaling, fill)
                for i in range(1, SLOTS)
            ]
            return [jnp.where(earlier, parts[0], parts[last])] + parts[1:last]

        scores = joint(q, keys, -1e30)
        top = functools.reduce(jnp.maximum, scores)
        top = jnp.max(top, -1, keepdims=True)
        raw = [jnp.exp(s - top) for s in scores]
        share = 1.0 / jnp.sum(functools.reduce(jnp.add, raw), -1, keepdims=True)
        probs = [r * share for r in raw]
        grads = joint(g, vals, None)
        delta = functools.reduce(jnp.add, [p * d for p, d in zip(probs, grads)])
        delta = jnp.sum(delta, -1, keepdims=True)
        for ref, parts in (
            (low_all, probs),
            (score_all, [p * (d - delta) * scaling for p, d in zip(probs, grads)]),
        ):
            ref[rows, :TOK] = jnp.where(earlier, parts[0], 0.0).astype(BF16)
            ref[rows, last * TOK :] = jnp.where(earlier, 0.0, parts[0]).astype(BF16)
            for i in range(1, last):
                ref[rows, i * TOK : (i + 1) * TOK] = parts[i].astype(BF16)
        out_ref[:, h * HD : (h + 1) * HD] = dot(low_all[rows, :], vals[...], NN).astype(BF16)
        out_ref[:, WIDE + h * HD : WIDE + (h + 1) * HD] = turn(
            dot(score_all[rows, :], keys[...], NN), cos_ref[:TOK, :], -sin_ref[:TOK, :]
        ).astype(BF16)
    for i in range(SLOTS):
        cols = slice(i * TOK, (i + 1) * TOK)
        part_key = dot(score_all[:, cols], q_all[...], TN)
        part_value = dot(low_all[:TOK, cols], qg_ref[:, WIDE : WIDE + HD], TN) + dot(
            low_all[TOK:, cols], qg_ref[:, WIDE + HD :], TN
        )
        keep_ref[cols, :] = jnp.where(is_key, part_key, part_value).astype(BF16)
        give_ref[cols, :] = jnp.where(is_key, part_value, part_key).astype(BF16)


def call_attend(table, query_grad, cosine, sine, other, sources):
    return pl.pallas_call(
        attend_kernel,
        compiler_params=room(24),
        out_shape=(
            jax.ShapeDtypeStruct((TOK, 2 * WIDE), BF16),
            jax.ShapeDtypeStruct((KEYS, HD), BF16),
            jax.ShapeDtypeStruct((KEYS, HD), BF16),
        ),
        in_specs=[SMEM] + [VMEM] * (4 + len(sources)),
        out_specs=(VMEM,) * 3,
        scratch_shapes=[
            pltpu.VMEM((KEYS, HD), BF16),
            pltpu.VMEM((KEYS, HD), BF16),
            pltpu.VMEM((KEYS, HD), BF16),
            pltpu.VMEM((2 * TOK, HD), BF16),
            pltpu.VMEM((2 * TOK, KEYS), BF16),
            pltpu.VMEM((2 * TOK, KEYS), BF16),
        ],
    )(table, query_grad, cosine, sine, other, *sources)


def spread_kernel(table, keep_ref, got_ref, *refs):
    outs, total = refs[:-1], refs[-1]
    total[...] = jnp.zeros_like(total)
    for source, offset in ((keep_ref, OWN), (got_ref, OTHER)):
        for i in range(SLOTS):
            at = pl.ds(pl.multiple_of(table[offset + i] * TOK, TOK), TOK)
            total[at, :] += source[i * TOK : (i + 1) * TOK, :].astype(F32)
    for k in range(CHIPS):
        outs[k][...] = total[k * PAIR : (k + 1) * PAIR, :].astype(outs[k].dtype)
        low = CHIPS * PAIR + k * TOK
        outs[CHIPS + k][...] = total[low : low + TOK, :].astype(BF16)


def call_spread(table, keep, got):
    return pl.pallas_call(
        spread_kernel,
        compiler_params=room(12),
        out_shape=tuple(
            [jax.ShapeDtypeStruct((PAIR, HD), F32)]
            + [jax.ShapeDtypeStruct((PAIR, HD), BF16)] * (CHIPS - 1)
            + [jax.ShapeDtypeStruct((TOK, HD), BF16)] * CHIPS
        ),
        in_specs=[SMEM, VMEM, VMEM],
        out_specs=(VMEM,) * (2 * CHIPS),
        scratch_shapes=[
            pltpu.VMEM((CHIPS * PAIR + CHIPS * TOK, HD), F32),
        ],
    )(table, keep, got)


def sum_kernel(*refs):
    total = refs[0][...].astype(F32)
    for ref in refs[1:-1]:
        total = total + ref[...].astype(F32)
    refs[-1][...] = total.astype(refs[-1].dtype)


def call_sum(parts, dtype):
    return pl.pallas_call(
        sum_kernel,
        compiler_params=room(6),
        out_shape=jax.ShapeDtypeStruct(parts[0].shape, dtype),
        in_specs=[VMEM] * len(parts),
        out_specs=VMEM,
    )(*parts)


def close_kernel(table, own_ref, *refs):
    backs = refs[:-4]
    cos_ref, sin_ref, o_ref, total = refs[-4:]
    total[...] = own_ref[...]
    for k, back in enumerate(backs):
        code = table[LAND + k]

        @pl.when(code < CORES)
        def _(back=back, code=code):
            at = pl.ds(pl.multiple_of(code * TOK, TOK), TOK)
            total[at, :] += back[...].astype(F32)

    is_key = table[CORE] == 0

    @pl.when(is_key)
    def _():
        o_ref[...] = turn(total[...], cos_ref[...], -sin_ref[...]).astype(BF16)

    @pl.when(jnp.logical_not(is_key))
    def _():
        o_ref[...] = total[...].astype(BF16)


def call_close(table, own, backs, cosine, sine):
    return pl.pallas_call(
        close_kernel,
        compiler_params=room(8),
        out_shape=jax.ShapeDtypeStruct((PAIR, HD), BF16),
        in_specs=[SMEM] + [VMEM] * (3 + len(backs)),
        out_specs=VMEM,
        scratch_shapes=[pltpu.VMEM((PAIR, HD), F32)],
    )(table, own, *backs, cosine, sine)


def along(block, shift, starts=range(CHIPS)):
    return lax.ppermute(block, "chip", [(i, i + shift) for i in starts if 0 <= i + shift < CHIPS])


def next_row(block, shift):
    rows = lax.axis_size("row")
    return lax.ppermute(
        block, "row", [(i, i + shift) for i in range(rows) if 0 <= i + shift < rows]
    )


def swap(block):
    return lax.ppermute(block, "core", [(0, 1), (1, 0)])


def shards(queries, keys, values, grad_attn, parent_gap):
    tokens = queries.shape[0]
    chunks = [
        x.reshape(tokens, HEADS, HD).transpose(1, 0, 2) for x in (keys, values)
    ]
    both = lax.all_to_all(
        jnp.concatenate(chunks, 0), ("core", "head"), split_axis=0, concat_axis=0, tiled=True
    ).reshape(PAIR, HD)
    table = call_plan(parent_gap)
    slot_angles = angles_of(table[DEPTHS : DEPTHS + SLOTS])
    slot_cos, slot_sin = jnp.cos(slot_angles), jnp.sin(slot_angles)
    both, slot_cos, slot_sin = lax.optimization_barrier((both, slot_cos, slot_sin))
    near, far = call_give(table, both)
    pairs = [both, along(near, -1), along(far, -2, (2,))]
    query_grad = jnp.concatenate(
        [queries.reshape(tokens, HEADS, WIDE), grad_attn.reshape(tokens, HEADS, WIDE)], 2
    ).reshape(tokens, HEADS * 2 * WIDE)
    query_grad = lax.all_to_all(query_grad, "head", split_axis=1, concat_axis=0, tiled=True)
    held = call_pick(table, pairs, SEND, 1)
    relay = next_row(held, 1)
    relay, query_grad = lax.optimization_barrier((relay, query_grad))
    sources = [both] + [along(both, k) for k in (1, 2, 3)]
    sources += [relay] + [along(relay, -k) for k in (1, 2, 3)]
    other = swap(call_pick(table, sources, OTHER, SLOTS))
    out, keep, give = call_attend(table, query_grad, slot_cos, slot_sin, other, sources)
    got = swap(give)
    out = lax.all_to_all(out, "head", split_axis=0, concat_axis=1, tiled=True)
    spread = call_spread(table, keep, got)
    own, within, stack = spread[0], spread[1:CHIPS], spread[CHIPS:]
    stack_sum = call_sum([stack[0]] + [along(stack[k], k) for k in (1, 2, 3)], BF16)
    stack_sum, late_table = lax.optimization_barrier((stack_sum, table))
    back = next_row(stack_sum, -1)
    pair_angles = angles_of(late_table[PAIRS : PAIRS + CORES])
    pair_cos, pair_sin = jnp.cos(pair_angles), jnp.sin(pair_angles)
    back, pair_cos, pair_sin = lax.optimization_barrier((back, pair_cos, pair_sin))
    own = call_sum([own] + [along(within[k - 1], -k) for k in (1, 2, 3)], F32)
    backs = [back, along(back, 1), along(back, 2, (0,))]
    grad_both = call_close(table, own, backs, pair_cos, pair_sin)
    grad_both, out = lax.optimization_barrier((grad_both, out))
    grad_both = lax.all_to_all(
        grad_both.reshape(CORES * HEADS, tokens, HD),
        ("core", "head"),
        split_axis=0,
        concat_axis=0,
        tiled=True,
    )
    grad_key, grad_value = (
        x.transpose(1, 0, 2).reshape(tokens, HEADS * HD)
        for x in (grad_both[:HEADS], grad_both[HEADS:])
    )
    out = out.reshape(tokens, HEADS, 2, WIDE)
    attended = out[:, :, 0].reshape(tokens, HEADS * WIDE)
    grad_query = out[:, :, 1].reshape(tokens, HEADS * WIDE)
    return attended, grad_query, grad_key, grad_value


def solution(mesh):
    devices = mesh.devices
    rows = devices.shape[0] // ROW
    split = Mesh(
        devices.reshape(rows, CHIPS, CORES, devices.shape[1]), ("row", "chip", "core", "head")
    )
    spec = P(("row", "chip", "core", "head"), None)

    return jax.shard_map(
        shards,
        mesh=split,
        in_specs=(spec, spec, spec, spec, P()),
        out_specs=(spec, spec, spec, spec),
        check_vma=False,
    )
```

```python
import functools
import math

import jax
import jax.numpy as jnp
from jax import lax
from jax.experimental import pallas as pl
from jax.experimental.pallas import tpu as pltpu
from jax.sharding import Mesh
from jax.sharding import PartitionSpec as P


HD = 256
HALF = HD // 2
TOK = 256
LEVELS = 4
SLOTS = LEVELS + 1
CHIPS = 4
CORES = 2
PAIR = CORES * TOK
KEYS = SLOTS * TOK
ROW = CHIPS * CORES
HEADS = 4
WIDE = 2 * HD
OWN, OTHER, SEEN, SEND, LAND, CORE, DEPTHS, PAIRS, TABLE = 0, 5, 10, 14, 15, 18, 19, 24, 32
BASE = 10000.0
BF16 = jnp.bfloat16
F32 = jnp.float32

MIB = 1024 * 1024


def room(mib):
    return pltpu.CompilerParams(vmem_limit_bytes=mib * MIB)


VMEM = pl.BlockSpec(memory_space=pltpu.VMEM)
SMEM = pl.BlockSpec(memory_space=pltpu.SMEM)


def plan_kernel(gap_ref, table):
    row, chip, core = (lax.axis_index(name) for name in ("row", "chip", "core"))
    count = gap_ref.shape[0]
    first = row * ROW
    shard = first + chip * CORES + core
    pick = lambda cond, a, b: jnp.where(cond, a, b)

    def gap_of(node):
        inside = gap_ref[jnp.clip(node, 0, count - 1)]
        return pick(node >= count, 1, pick(node < 0, 0, inside))

    def elders_of(node):
        found = []
        for _ in range(LEVELS):
            gap = gap_of(node)
            node = pick(gap > 0, node - gap, -1)
            found.append(node)
        return found

    def deeper(node, depth):
        return depth + pick(gap_ref[node] == 1, 1, 0)

    depth = lax.fori_loop(0, first + chip * CORES + 1, deeper, jnp.int32(0))
    pair_depth = [depth, deeper(first + chip * CORES + 1, depth)]
    own_depth = pick(core == 0, pair_depth[0], pair_depth[1])
    stack, relay = elders_of(first), elders_of(first + ROW)
    for start, node, half in (
        (OWN, shard, core),
        (OTHER, shard + 1 - 2 * core, 1 - core),
    ):
        table[start] = half
        for i, elder in enumerate(elders_of(node)):
            in_row = 2 * (chip - ((elder - first) >> 1)) + (elder & 1)
            before = jnp.int32(0)
            for j in range(LEVELS):
                before = pick(elder == stack[j], 3 * CHIPS - 1 - j - chip, before)
            code = pick(elder < 0, 0, pick(elder >= first, in_row, before))
            table[start + 1 + i] = jnp.clip(code, 0, 3 * CHIPS - 1)
            if start == OWN:
                table[SEEN + i] = pick(elder >= 0, 1, 0)

    def held(rank):
        node = jnp.int32(-1)
        for j in range(LEVELS):
            node = pick(rank == j, relay[j], node)
        return node

    node = held(CHIPS - 1 - chip)
    code = 2 * (((node - first) >> 1) - chip) + (node & 1)
    table[SEND] = jnp.clip(code, 0, 2 * CHIPS - 3)
    for i, rank in enumerate((CHIPS - 1 - chip, CHIPS - chip, pick(chip == 2, CHIPS - 1, CHIPS))):
        node = held(rank)
        here = (node >= first) & (((node - first) >> 1) == chip)
        table[LAND + i] = pick(here, node & 1, CORES)
    table[CORE] = core
    for i in range(SLOTS):
        table[DEPTHS + i] = own_depth - i
    for i in range(CORES):
        table[PAIRS + i] = pair_depth[i]
    for i in range(PAIRS + CORES, TABLE):
        table[i] = 0


def call_plan(parent_gap):
    return pl.pallas_call(
        plan_kernel,
        out_shape=jax.ShapeDtypeStruct((TABLE,), jnp.int32),
        in_specs=[SMEM],
        out_specs=SMEM,
    )(parent_gap)


def angles_of(depth):
    frequency = jnp.exp(jnp.arange(HALF, dtype=F32) * (-2.0 * math.log(BASE) / HD))
    position = (depth[:, None] * TOK + jnp.arange(TOK, dtype=jnp.int32)[None, :]).reshape(-1)
    return position.astype(F32)[:, None] * frequency[None, :]


def turn(block, cosine, sine):
    first, second = block[:, :HALF], block[:, HALF:]
    return jnp.concatenate(
        [first * cosine - second * sine, second * cosine + first * sine], -1
    )


def fetch(code, sources, target):
    at = 0
    for ref in sources:
        for half in range(ref.shape[0] // TOK):

            @pl.when(code == at)
            def _(ref=ref, half=half):
                target[...] = ref[half * TOK : (half + 1) * TOK, :]

            at += 1


def part(ref, i):
    return ref.at[pl.ds(i * TOK, TOK)]


def pick_kernel(offset, number, table, *refs):
    sources, o_ref = refs[:-1], refs[-1]
    for i in range(number):
        fetch(table[offset + i], sources, part(o_ref, i))


def call_pick(table, sources, offset, number):
    return pl.pallas_call(
        functools.partial(pick_kernel, offset, number),
        compiler_params=room(4),
        out_shape=jax.ShapeDtypeStruct((number * TOK, HD), BF16),
        in_specs=[SMEM] + [VMEM] * len(sources),
        out_specs=VMEM,
    )(table, *sources)


NT = (((1,), (1,)), ((), ()))
NN = (((1,), (0,)), ((), ()))
TN = (((0,), (0,)), ((), ()))


def dot(a, b, dims):
    return lax.dot_general(a, b, dims, preferred_element_type=F32)


def attend_kernel(table, qg_ref, cos_ref, sin_ref, other_ref, *refs):
    sources = refs[: 2 * CHIPS]
    out_ref, keep_ref, give_ref = refs[2 * CHIPS : 2 * CHIPS + 3]
    mine_ref, keys, vals, q_all, low_all, score_all = refs[2 * CHIPS + 3 :]
    for i in range(SLOTS):
        fetch(table[OWN + i], sources, part(mine_ref, i))
    for h in range(2):
        q_all[h * TOK : (h + 1) * TOK, :] = turn(
            qg_ref[:, h * HD : (h + 1) * HD].astype(F32), cos_ref[:TOK, :], sin_ref[:TOK, :]
        ).astype(BF16)
    is_key = table[CORE] == 0
    for i in range(SLOTS):
        here = slice(i * TOK, (i + 1) * TOK)
        mine, other = mine_ref[here, :], other_ref[here, :]
        keys[here, :] = turn(
            jnp.where(is_key, mine, other).astype(F32), cos_ref[here, :], sin_ref[here, :]
        ).astype(BF16)
        vals[here, :] = jnp.where(is_key, other, mine)
    scaling = HD**-0.5
    earlier = lax.broadcasted_iota(jnp.int32, (TOK, TOK), 1) <= lax.broadcasted_iota(
        jnp.int32, (TOK, TOK), 0
    )
    last = SLOTS - 1
    block = lambda ref, i: ref[i * TOK : (i + 1) * TOK, :]
    for h in range(2):
        rows = slice(h * TOK, (h + 1) * TOK)
        q, g = q_all[rows, :], qg_ref[:, WIDE + h * HD : WIDE + (h + 1) * HD]

        def joint(a, which, fill):
            parts = [dot(a, block(which, i), NT) for i in range(SLOTS)]
            if fill is None:
                return [jnp.where(earlier, parts[0], parts[last])] + parts[1:last]
            parts = [parts[0] * scaling] + [
                jnp.where(table[SEEN + i - 1] > 0, parts[i] * scaling, fill)
                for i in range(1, SLOTS)
            ]
            return [jnp.where(earlier, parts[0], parts[last])] + parts[1:last]

        scores = joint(q, keys, -1e30)
        top = functools.reduce(jnp.maximum, scores)
        top = jnp.max(top, -1, keepdims=True)
        raw = [jnp.exp(s - top) for s in scores]
        share = 1.0 / jnp.sum(functools.reduce(jnp.add, raw), -1, keepdims=True)
        probs = [r * share for r in raw]
        grads = joint(g, vals, None)
        delta = functools.reduce(jnp.add, [p * d for p, d in zip(probs, grads)])
        delta = jnp.sum(delta, -1, keepdims=True)
        for ref, parts in (
            (low_all, probs),
            (score_all, [p * (d - delta) * scaling for p, d in zip(probs, grads)]),
        ):
            ref[rows, :TOK] = jnp.where(earlier, parts[0], 0.0).astype(BF16)
            ref[rows, last * TOK :] = jnp.where(earlier, 0.0, parts[0]).astype(BF16)
            for i in range(1, last):
                ref[rows, i * TOK : (i + 1) * TOK] = parts[i].astype(BF16)
        out_ref[:, h * HD : (h + 1) * HD] = dot(low_all[rows, :], vals[...], NN).astype(BF16)
        out_ref[:, WIDE + h * HD : WIDE + (h + 1) * HD] = turn(
            dot(score_all[rows, :], keys[...], NN), cos_ref[:TOK, :], -sin_ref[:TOK, :]
        ).astype(BF16)
    for i in range(SLOTS):
        cols = slice(i * TOK, (i + 1) * TOK)
        part_key = dot(score_all[:, cols], q_all[...], TN)
        part_value = dot(low_all[:TOK, cols], qg_ref[:, WIDE : WIDE + HD], TN) + dot(
            low_all[TOK:, cols], qg_ref[:, WIDE + HD :], TN
        )
        keep_ref[cols, :] = jnp.where(is_key, part_key, part_value).astype(BF16)
        give_ref[cols, :] = jnp.where(is_key, part_value, part_key).astype(BF16)


def call_attend(table, query_grad, cosine, sine, other, sources):
    return pl.pallas_call(
        attend_kernel,
        compiler_params=room(24),
        out_shape=(
            jax.ShapeDtypeStruct((TOK, 2 * WIDE), BF16),
            jax.ShapeDtypeStruct((KEYS, HD), BF16),
            jax.ShapeDtypeStruct((KEYS, HD), BF16),
        ),
        in_specs=[SMEM] + [VMEM] * (4 + len(sources)),
        out_specs=(VMEM,) * 3,
        scratch_shapes=[
            pltpu.VMEM((KEYS, HD), BF16),
            pltpu.VMEM((KEYS, HD), BF16),
            pltpu.VMEM((KEYS, HD), BF16),
            pltpu.VMEM((2 * TOK, HD), BF16),
            pltpu.VMEM((2 * TOK, KEYS), BF16),
            pltpu.VMEM((2 * TOK, KEYS), BF16),
        ],
    )(table, query_grad, cosine, sine, other, *sources)


def spread_kernel(table, keep_ref, got_ref, *refs):
    outs, total = refs[:-1], refs[-1]
    total[...] = jnp.zeros_like(total)
    for source, offset in ((keep_ref, OWN), (got_ref, OTHER)):
        for i in range(SLOTS):
            at = pl.ds(pl.multiple_of(table[offset + i] * TOK, TOK), TOK)
            total[at, :] += source[i * TOK : (i + 1) * TOK, :].astype(F32)
    for k in range(CHIPS):
        outs[k][...] = total[k * PAIR : (k + 1) * PAIR, :].astype(outs[k].dtype)
        low = CHIPS * PAIR + k * TOK
        outs[CHIPS + k][...] = total[low : low + TOK, :].astype(BF16)


def call_spread(table, keep, got):
    return pl.pallas_call(
        spread_kernel,
        compiler_params=room(12),
        out_shape=tuple(
            [jax.ShapeDtypeStruct((PAIR, HD), F32)]
            + [jax.ShapeDtypeStruct((PAIR, HD), BF16)] * (CHIPS - 1)
            + [jax.ShapeDtypeStruct((TOK, HD), BF16)] * CHIPS
        ),
        in_specs=[SMEM, VMEM, VMEM],
        out_specs=(VMEM,) * (2 * CHIPS),
        scratch_shapes=[
            pltpu.VMEM((CHIPS * PAIR + CHIPS * TOK, HD), F32),
        ],
    )(table, keep, got)


def sum_kernel(*refs):
    total = refs[0][...].astype(F32)
    for ref in refs[1:-1]:
        total = total + ref[...].astype(F32)
    refs[-1][...] = total.astype(refs[-1].dtype)


def call_sum(parts, dtype):
    return pl.pallas_call(
        sum_kernel,
        compiler_params=room(6),
        out_shape=jax.ShapeDtypeStruct(parts[0].shape, dtype),
        in_specs=[VMEM] * len(parts),
        out_specs=VMEM,
    )(*parts)


def close_kernel(table, own_ref, *refs):
    backs = refs[:-4]
    cos_ref, sin_ref, o_ref, total = refs[-4:]
    total[...] = own_ref[...]
    for k, back in enumerate(backs):
        code = table[LAND + k]

        @pl.when(code < CORES)
        def _(back=back, code=code):
            at = pl.ds(pl.multiple_of(code * TOK, TOK), TOK)
            total[at, :] += back[...].astype(F32)

    is_key = table[CORE] == 0

    @pl.when(is_key)
    def _():
        o_ref[...] = turn(total[...], cos_ref[...], -sin_ref[...]).astype(BF16)

    @pl.when(jnp.logical_not(is_key))
    def _():
        o_ref[...] = total[...].astype(BF16)


def call_close(table, own, backs, cosine, sine):
    return pl.pallas_call(
        close_kernel,
        compiler_params=room(8),
        out_shape=jax.ShapeDtypeStruct((PAIR, HD), BF16),
        in_specs=[SMEM] + [VMEM] * (3 + len(backs)),
        out_specs=VMEM,
        scratch_shapes=[pltpu.VMEM((PAIR, HD), F32)],
    )(table, own, *backs, cosine, sine)


def along(block, shift, starts=range(CHIPS)):
    return lax.ppermute(block, "chip", [(i, i + shift) for i in starts if 0 <= i + shift < CHIPS])


def next_row(block, shift):
    rows = lax.axis_size("row")
    return lax.ppermute(
        block, "row", [(i, i + shift) for i in range(rows) if 0 <= i + shift < rows]
    )


def swap(block):
    return lax.ppermute(block, "core", [(0, 1), (1, 0)])


def shards(queries, keys, values, grad_attn, parent_gap):
    tokens = queries.shape[0]
    chunks = [
        x.reshape(tokens, HEADS, HD).transpose(1, 0, 2) for x in (keys, values)
    ]
    both = lax.all_to_all(
        jnp.concatenate(chunks, 0), ("core", "head"), split_axis=0, concat_axis=0, tiled=True
    ).reshape(PAIR, HD)
    table = call_plan(parent_gap)
    slot_angles = angles_of(table[DEPTHS : DEPTHS + SLOTS])
    slot_cos, slot_sin = jnp.cos(slot_angles), jnp.sin(slot_angles)
    both, slot_cos, slot_sin = lax.optimization_barrier((both, slot_cos, slot_sin))
    pairs = [both, along(both, -1), along(both, -2, (2,))]
    query_grad = jnp.concatenate(
        [queries.reshape(tokens, HEADS, WIDE), grad_attn.reshape(tokens, HEADS, WIDE)], 2
    ).reshape(tokens, HEADS * 2 * WIDE)
    query_grad = lax.all_to_all(query_grad, "head", split_axis=1, concat_axis=0, tiled=True)
    held = call_pick(table, pairs, SEND, 1)
    relay = next_row(held, 1)
    relay, query_grad = lax.optimization_barrier((relay, query_grad))
    sources = [both] + [along(both, k) for k in (1, 2, 3)]
    sources += [relay] + [along(relay, -k) for k in (1, 2, 3)]
    other = swap(call_pick(table, sources, OTHER, SLOTS))
    out, keep, give = call_attend(table, query_grad, slot_cos, slot_sin, other, sources)
    got = swap(give)
    out = lax.all_to_all(out, "head", split_axis=0, concat_axis=1, tiled=True)
    spread = call_spread(table, keep, got)
    own, within, stack = spread[0], spread[1:CHIPS], spread[CHIPS:]
    stack_sum = call_sum([stack[0]] + [along(stack[k], k) for k in (1, 2, 3)], BF16)
    stack_sum, late_table = lax.optimization_barrier((stack_sum, table))
    back = next_row(stack_sum, -1)
    pair_angles = angles_of(late_table[PAIRS : PAIRS + CORES])
    pair_cos, pair_sin = jnp.cos(pair_angles), jnp.sin(pair_angles)
    back, pair_cos, pair_sin = lax.optimization_barrier((back, pair_cos, pair_sin))
    own = call_sum([own] + [along(within[k - 1], -k) for k in (1, 2, 3)], F32)
    backs = [back, along(back, 1), along(back, 2, (0,))]
    grad_both = call_close(table, own, backs, pair_cos, pair_sin)
    grad_both, out = lax.optimization_barrier((grad_both, out))
    grad_both = lax.all_to_all(grad_both, ("core", "head"), split_axis=0, concat_axis=1, tiled=True)
    out = out.reshape(tokens, HEADS, 2, WIDE)
    attended = out[:, :, 0].reshape(tokens, HEADS * WIDE)
    grad_query = out[:, :, 1].reshape(tokens, HEADS * WIDE)
    half = HEADS * HD
    return attended, grad_query, grad_both[:, :half], grad_both[:, half:]


def solution(mesh):
    devices = mesh.devices
    rows = devices.shape[0] // ROW
    split = Mesh(
        devices.reshape(rows, CHIPS, CORES, devices.shape[1]), ("row", "chip", "core", "head")
    )
    spec = P(("row", "chip", "core", "head"), None)

    return jax.shard_map(
        shards,
        mesh=split,
        in_specs=(spec, spec, spec, spec, P()),
        out_specs=(spec, spec, spec, spec),
        check_vma=False,
    )
```
